256 devices in a mesh: pipe: 2 (over core), ctx: 128 (over z, y, x).
Axes of the slice: x: 4, y: 4, z: 8, core: 2. Of those that a mesh axis runs over, the one named last changes fastest.
Arguments:
- t_query: bfloat16 [2, 16384, 4096], P('pipe', 'ctx'), may hold values from -33 to 33
- t_key: bfloat16 [2, 16384, 512], P('pipe', 'ctx'), may hold values from -6 to 6
- t_value: bfloat16 [2, 16384, 512], P('pipe', 'ctx'), may hold values from -6 to 6
- s_query: bfloat16 [2, 16384, 4096], P('pipe', 'ctx'), may hold values from -33 to 33
- s_key: bfloat16 [2, 16384, 512], P('pipe', 'ctx'), may hold values from -6 to 6
- s_value: bfloat16 [2, 16384, 512], P('pipe', 'ctx'), may hold values from -6 to 6
- segment_ids: int32 [16384], replicated, may hold values from 0 to 127, never falling along the last dimension, each value on 1 to 256 neighbouring positions
Outputs:
- loss: float32 [], replicated
- query_grad: float32 [2, 16384, 4096], P('pipe', 'ctx')
- key_grad: float32 [2, 16384, 512], P('pipe', 'ctx')
- value_grad: float32 [2, 16384, 512], P('pipe', 'ctx')
The draws below stay inside these ranges and needn't reach their ends.
Inputs may be any that keep to these rules, and one draw needn't show every extreme that they name: `segment_ids`: segment ids never fall along the tokens; a document holds at most 256 tokens, and one holds exactly that many.
All inputs are finite; a program needn't handle non-finite values.
Results may differ from the reference program's by a relative error of at most 0.006.
Values may be sent and summed in bfloat16 or wider, within the bound.
No kernel may reach another device: no remote copies, remote signals or barrier semaphores. Data moves between devices by JAX's collectives and lax.ppermute only.
A program may use at most 128 MiB of HBM per device.

```python
import math
import jax
import jax.numpy as jnp
import numpy as np
from jax import lax

TOK_DEV = 128
REACH = 2
HEADS = 32
KV_HEADS = 4
HEAD_DIM = 128
SECTIONS = 2
TOKENS = 16384


def drawn_pair(key, tag):
    base = jax.random.fold_in(key, tag)
    key_first, key_second = jax.random.split(base)
    group = HEADS // KV_HEADS
    shape_query = (SECTIONS, TOKENS, KV_HEADS, group, HEAD_DIM)
    shape_keys = (SECTIONS, TOKENS, KV_HEADS, HEAD_DIM)
    keys = jnp.clip(jax.random.normal(key_first, shape_keys, jnp.float32), -6.0, 6.0)
    query = jnp.clip(jax.random.normal(key_second, shape_query, jnp.float32), -6.0, 6.0)
    return (query.reshape(SECTIONS, TOKENS, HEADS * HEAD_DIM).astype(jnp.bfloat16), keys.reshape(SECTIONS, TOKENS, KV_HEADS * HEAD_DIM).astype(jnp.bfloat16))


def draw_t_query(key, part):
    return drawn_pair(key, 11)[0]


def draw_t_key(key, part):
    return drawn_pair(key, 11)[1]


def draw_s_query(key, part):
    return drawn_pair(key, 23)[0]


def draw_s_key(key, part):
    return drawn_pair(key, 23)[1]


def levels(own_key, dims, cuts, low, top_value):
    gain = 1.0
    for position, blocks in cuts:
        heights = jax.random.uniform(jax.random.fold_in(jax.random.fold_in(own_key, 6), position), (blocks,), jnp.float32, low / len(cuts), top_value / len(cuts))
        gain = gain * jnp.repeat(jnp.exp(heights), dims[position] // blocks).reshape((-1,) + (1,) * (len(dims) - 1 - position))
    return gain


def split_up(count, total, bound, lean):
    weights = [(1 << 20) // math.isqrt(grade ** lean) + 1 for grade in range(2, count + 1)]
    spare, given = total - bound - (count - 1), [1] * (count - 1)
    while spare > 0:
        free = [i for i in range(count - 1) if given[i] < bound]
        pool, left = sum([weights[i] for i in free]), spare
        for i in free:
            addition = min(bound - given[i], max(1, left * weights[i] // pool), spare)
            given[i] = given[i] + addition
            spare = spare - addition
    return np.array([bound] + given)


def ragged_sizes(stream_key, count, total, limit, slope):
    if count == 2:
        one = jax.random.randint(stream_key, (), max(1, total - limit), min(limit, total - 1) + 1)
        return jnp.stack([one, total - one])
    tallies = jnp.asarray(split_up(count, total, limit, slope), jnp.int32)
    pairs = (count - 1) // 2
    source_of, receiver = tallies[1:1 + 2 * pairs:2], tallies[2:2 + 2 * pairs:2]
    slack = jnp.minimum(source_of - 1, limit - receiver)
    passed = jax.random.randint(jax.random.fold_in(stream_key, 1), (pairs,), 0, 1 << 20) % (slack + 1)
    tallies = tallies.at[1:1 + 2 * pairs:2].set(source_of - passed).at[2:2 + 2 * pairs:2].set(receiver + passed)
    return tallies[jax.random.permutation(jax.random.fold_in(stream_key, 2), count)]


def scatter_about(rng, dims, width, bound, pieces=(), held_as=jnp.bfloat16):
    values = width * jax.random.normal(rng, dims, jnp.float32)
    if pieces:
        values = values * levels(rng, dims, pieces, -0.22, 0.18)
    return jnp.clip(values, -bound, bound).astype(held_as)


def setup_inputs(seed: int = 0) -> dict:
    streams_of = jax.random.split(jax.random.key(seed), 8)
    t_query = draw_t_query(jax.random.fold_in(streams_of[7], 71), 0)
    t_key = draw_t_key(jax.random.fold_in(streams_of[7], 71), 0)
    t_value = scatter_about(streams_of[2], (SECTIONS, TOKENS, KV_HEADS * HEAD_DIM), 1.0, 6.0, ((0, 2), (1, 128)))
    s_query = draw_s_query(jax.random.fold_in(streams_of[7], 71), 0)
    s_key = draw_s_key(jax.random.fold_in(streams_of[7], 71), 0)
    s_value = scatter_about(streams_of[5], (SECTIONS, TOKENS, KV_HEADS * HEAD_DIM), 1.0, 6.0, ((0, 2), (1, 128)))
    segment_ids = jnp.searchsorted(jnp.cumsum(ragged_sizes(streams_of[6], TOKENS // TOK_DEV, TOKENS, REACH * TOK_DEV, 1)), jnp.arange(TOKENS), side="right").astype(jnp.int32)
    return dict(t_query=t_query, t_key=t_key, t_value=t_value, s_query=s_query, s_key=s_key, s_value=s_value, segment_ids=segment_ids)


NEG_FILL = -1e+30

def attend(query_half, keys_half, values_half, allowed):
    tok_rows = query_half.shape[0]
    key_count = keys_half.shape[0]
    group = HEADS // KV_HEADS
    query_heads = query_half.reshape(tok_rows, KV_HEADS, group, HEAD_DIM).astype(jnp.float32)
    key_heads = keys_half.reshape(key_count, KV_HEADS, HEAD_DIM).astype(jnp.float32)
    value_heads = values_half.reshape(key_count, KV_HEADS, HEAD_DIM).astype(jnp.float32)
    scores = jnp.einsum('rkgd,wkd->kgrw', query_heads, key_heads) * HEAD_DIM ** (-0.5)
    scores = jnp.where(allowed[None, None], scores, NEG_FILL)
    row_peak = lax.optimization_barrier(jnp.max(scores, axis=-1, keepdims=True))
    expo = jnp.exp(scores - row_peak)
    row_total = lax.optimization_barrier(jnp.sum(expo, axis=-1, keepdims=True))
    weights = lax.optimization_barrier(expo.astype(jnp.bfloat16)).astype(jnp.float32)
    mixed = jnp.einsum('kgrw,wkd->rkgd', weights, value_heads) / jnp.transpose(row_total, (2, 0, 1, 3))
    return (mixed.reshape(tok_rows, HEADS * HEAD_DIM).astype(jnp.bfloat16), expo, row_total)

def attend_grad(query_half, keys_half, values_half, allowed, out_half, out_grad):
    tok_rows = query_half.shape[0]
    key_count = keys_half.shape[0]
    group = HEADS // KV_HEADS
    scale = HEAD_DIM ** (-0.5)
    unused_out, expo, row_total = attend(query_half, keys_half, values_half, allowed)
    query_heads = query_half.reshape(tok_rows, KV_HEADS, group, HEAD_DIM).astype(jnp.float32)
    key_heads = keys_half.reshape(key_count, KV_HEADS, HEAD_DIM).astype(jnp.float32)
    value_heads = values_half.reshape(key_count, KV_HEADS, HEAD_DIM).astype(jnp.float32)
    prob = expo / row_total
    prob_half = lax.optimization_barrier(prob.astype(jnp.bfloat16)).astype(jnp.float32)
    grad_half = lax.optimization_barrier(out_grad.astype(jnp.bfloat16)).astype(jnp.float32)
    grad_heads = grad_half.reshape(tok_rows, KV_HEADS, group, HEAD_DIM)
    out_heads = out_half.astype(jnp.float32).reshape(tok_rows, KV_HEADS, group, HEAD_DIM)
    value_win = jnp.einsum('kgrw,rkgd->wkd', prob_half, grad_heads)
    dprob = jnp.einsum('rkgd,wkd->kgrw', grad_heads, value_heads)
    delta = jnp.transpose(lax.optimization_barrier(jnp.sum(grad_heads * out_heads, axis=-1)), (1, 2, 0))
    dscore = prob * (dprob - delta[..., None])
    dscore = lax.optimization_barrier(dscore.astype(jnp.bfloat16)).astype(jnp.float32)
    query_grad = jnp.einsum('kgrw,wkd->rkgd', dscore, key_heads) * scale
    key_win = jnp.einsum('kgrw,rkgd->wkd', dscore, query_heads) * scale
    return (query_grad.reshape(tok_rows, HEADS * HEAD_DIM), key_win.reshape(key_count, KV_HEADS * HEAD_DIM), value_win.reshape(key_count, KV_HEADS * HEAD_DIM))

def reference(t_query, t_key, t_value, s_query, s_key, s_value, segment_ids):
    tok_rows = TOK_DEV
    key_pad = REACH * tok_rows
    key_span = key_pad + tok_rows
    key_width = KV_HEADS * HEAD_DIM
    seg_front = jnp.concatenate([jnp.full((key_pad,), -1, jnp.int32), segment_ids])
    causal = jnp.arange(key_span)[None, :] <= jnp.arange(tok_rows)[:, None] + key_pad
    starts = jnp.arange(TOKENS // tok_rows, dtype=jnp.int32) * tok_rows

    def allowed_at(start):
        key_seg = lax.dynamic_slice_in_dim(seg_front, start, key_span)
        query_seg = lax.dynamic_slice_in_dim(segment_ids, start, tok_rows)
        return (key_seg[None, :] == query_seg[:, None]) & causal

    def padded(keys):
        return jnp.concatenate([jnp.zeros((key_pad, key_width), keys.dtype), keys], axis=0)

    def section_forward(query, keys, values):
        keys_pad = padded(keys)
        values_pad = padded(values)

        def one_block(start):
            block_query = lax.dynamic_slice_in_dim(query, start, tok_rows)
            block_keys = lax.dynamic_slice_in_dim(keys_pad, start, key_span)
            block_values = lax.dynamic_slice_in_dim(values_pad, start, key_span)
            result, unused_expo, unused_total = attend(block_query, block_keys, block_values, allowed_at(start))
            return result
        return lax.map(one_block, starts).reshape(TOKENS, HEADS * HEAD_DIM)

    def section_backward(query, keys, values, out_half, out_grad):
        keys_pad = padded(keys)
        values_pad = padded(values)

        def one_block(carry, start):
            key_acc, value_acc = carry
            block_query = lax.dynamic_slice_in_dim(query, start, tok_rows)
            block_keys = lax.dynamic_slice_in_dim(keys_pad, start, key_span)
            block_values = lax.dynamic_slice_in_dim(values_pad, start, key_span)
            block_out = lax.dynamic_slice_in_dim(out_half, start, tok_rows)
            block_grad = lax.dynamic_slice_in_dim(out_grad, start, tok_rows)
            query_part, key_part, value_part = attend_grad(block_query, block_keys, block_values, allowed_at(start), block_out, block_grad)
            key_acc = lax.dynamic_update_slice_in_dim(key_acc, lax.dynamic_slice_in_dim(key_acc, start, key_span) + key_part, start, 0)
            value_acc = lax.dynamic_update_slice_in_dim(value_acc, lax.dynamic_slice_in_dim(value_acc, start, key_span) + value_part, start, 0)
            return ((key_acc, value_acc), query_part)
        empty = jnp.zeros((TOKENS + key_pad, key_width), jnp.float32)
        (key_acc, value_acc), query_parts = lax.scan(one_block, (empty, empty), starts)
        return (query_parts.reshape(TOKENS, HEADS * HEAD_DIM), key_acc[key_pad:], value_acc[key_pad:])
    teacher_outs = [section_forward(t_query[p], t_key[p], t_value[p]) for p in range(SECTIONS)]
    student_outs = [section_forward(s_query[p], s_key[p], s_value[p]) for p in range(SECTIONS)]
    zeros_full = jnp.zeros((TOKENS, HEADS * HEAD_DIM), jnp.float32)
    student_sum = zeros_full
    teacher_cum = zeros_full
    gaps = []
    for p in range(SECTIONS):
        student_sum = student_sum + student_outs[p].astype(jnp.float32)
        teacher_cum = teacher_cum + teacher_outs[p].astype(jnp.float32)
        if p + 1 < SECTIONS:
            ahead = teacher_outs[p + 1].astype(jnp.float32)
        else:
            ahead = zeros_full
        gaps.append(student_sum - (teacher_cum + ahead))
    squares = jnp.zeros((), jnp.float32)
    for p in range(SECTIONS):
        squares = squares + jnp.sum(gaps[p] * gaps[p])
    loss = squares / float(SECTIONS * TOKENS * HEADS * HEAD_DIM)
    running = zeros_full
    query_list = [None] * SECTIONS
    key_list = [None] * SECTIONS
    value_list = [None] * SECTIONS
    for p in reversed(range(SECTIONS)):
        running = running + gaps[p]
        query_list[p], key_list[p], value_list[p] = section_backward(s_query[p], s_key[p], s_value[p], student_outs[p], running)
    return (loss, jnp.stack(query_list), jnp.stack(key_list), jnp.stack(value_list))
```

```python
import functools
import jax
import jax.numpy as jnp
from jax import lax
from jax.experimental import pallas as pl
from jax.experimental.pallas import tpu as pltpu
from jax.sharding import PartitionSpec as P

REACH = 2
HEADS = 32
KV_HEADS = 4
HEAD_DIM = 128
GROUP = HEADS // KV_HEADS
TOK = 128
SPAN = (REACH + 1) * TOK
PARTS = 2
PGROUPS = KV_HEADS // PARTS
PW = PGROUPS * HEAD_DIM
PQ = PGROUPS * GROUP * HEAD_DIM
PAIR = 2

NEG_FILL = -1e30
SCALE = HEAD_DIM ** (-0.5)
LOG2E = 1.4426950408889634
EXP_SCALE = SCALE * LOG2E
NT = (((1,), (1,)), ((), ()))
NN = (((1,), (0,)), ((), ()))
TN = (((0,), (0,)), ((), ()))


def mm(a, b, dims):
    return lax.dot_general(a, b, dims, preferred_element_type=jnp.float32)


def rotate(block, axis, distance):
    count = lax.axis_size(axis)
    return lax.ppermute(block, axis, [(i, (i + distance) % count) for i in range(count)])


def pack_body(pos_ref, tk, tv, sk, sv, seg0, seg1, seg2, *outs):
    packs, bias = outs[:PARTS], outs[PARTS]
    for p in range(PARTS):
        for m, src in enumerate((tk, tv, sk, sv)):
            packs[p][m] = src[0, :, p * PW : (p + 1) * PW]
    own = seg0[0].astype(jnp.float32)
    queries = jnp.broadcast_to(own, (TOK, TOK))
    for k, seg in enumerate((seg2, seg1, seg0)):
        keys = jnp.broadcast_to(seg[0].astype(jnp.float32), (TOK, TOK)).T
        ok = keys == queries
        if k == REACH:
            row = lax.broadcasted_iota(jnp.int32, (TOK, TOK), 0)
            col = lax.broadcasted_iota(jnp.int32, (TOK, TOK), 1)
            ok = ok & (row <= col)
        bias[k * TOK : (k + 1) * TOK, :] = jnp.where(ok, 0.0, NEG_FILL)


def pack(pos, blocks, segment_ids):
    count = segment_ids.shape[0] // TOK
    seg = segment_ids.reshape(count, 1, TOK)
    kv = pl.BlockSpec((1, TOK, KV_HEADS * HEAD_DIM), lambda i, pos: (0, 0, 0))
    segs = [
        pl.BlockSpec((1, 1, TOK), lambda i, pos, d=d: (lax.rem(pos[0] + count - d, count), 0, 0))
        for d in range(REACH + 1)
    ]
    whole = lambda *shape: pl.BlockSpec(shape, lambda i, pos: (0,) * len(shape))
    return pl.pallas_call(
        pack_body,
        grid_spec=pltpu.PrefetchScalarGridSpec(
            num_scalar_prefetch=1,
            grid=(1,),
            in_specs=[kv] * 4 + segs,
            out_specs=[whole(4, TOK, PW)] * PARTS + [whole(SPAN, TOK)],
        ),
        out_shape=[jax.ShapeDtypeStruct((4, TOK, PW), jnp.bfloat16)] * PARTS
        + [jax.ShapeDtypeStruct((SPAN, TOK), jnp.float32)],
        name="pack",
    )(pos, *blocks, seg, seg, seg)


def stacked(q_ref, pair):
    first = pair * PAIR
    return jnp.concatenate(
        [q_ref[0, :, (first + j) * HEAD_DIM : (first + j + 1) * HEAD_DIM] for j in range(PAIR)],
        axis=0,
    )


def forward_body(stage_ref, tq, sq, own, nb1, nb2, bias, s_out, t_out, send, lse):
    ahead = stage_ref[0].astype(jnp.float32) + 1.0
    mask = jnp.concatenate([bias[...]] * PAIR, axis=1)
    models = []
    for base in (0, 2):
        keys = jnp.concatenate([nb2[base], nb1[base], own[base]], axis=0)
        values = jnp.concatenate(
            [nb2[base + 1].T, nb1[base + 1].T, own[base + 1].T], axis=1
        )
        models.append((keys, values))
    for pair in range(GROUP // PAIR):
        outs = []
        for model, q_ref in enumerate((tq, sq)):
            keys, values = models[model]
            scores = mm(keys, stacked(q_ref, pair), NT) + mask
            peak = jnp.max(scores, axis=0, keepdims=True)
            expo = jnp.exp2((scores - peak) * EXP_SCALE)
            total = jnp.sum(expo, axis=0, keepdims=True)
            mixed = mm(values, expo.astype(jnp.bfloat16), NN) / total
            outs.append(mixed.astype(jnp.bfloat16))
            if model == 1:
                level = peak * EXP_SCALE + jnp.log2(total)
        t_half, s_half = outs
        diff = (s_half.astype(jnp.float32) - ahead * t_half.astype(jnp.float32)).astype(jnp.bfloat16)
        for j in range(PAIR):
            h = pair * PAIR + j
            rows, cols = pl.ds(h * HEAD_DIM, HEAD_DIM), slice(j * TOK, (j + 1) * TOK)
            s_out[rows, :] = s_half[:, cols]
            t_out[rows, :] = t_half[:, cols]
            send[rows, :] = diff[:, cols]
            lse[h : h + 1, :] = level[:, cols]


def forward(part, stage, t_query, s_query, own, nb1, nb2, bias):
    width = GROUP * HEAD_DIM
    query = pl.BlockSpec((1, TOK, width), lambda g, st: (0, 0, part * PGROUPS + g))
    kv = pl.BlockSpec((4, TOK, HEAD_DIM), lambda g, st: (0, 0, g))
    flipped = pl.BlockSpec((width, TOK), lambda g, st: (g, 0))
    half = jax.ShapeDtypeStruct((PQ, TOK), jnp.bfloat16)
    return pl.pallas_call(
        forward_body,
        grid_spec=pltpu.PrefetchScalarGridSpec(
            num_scalar_prefetch=1,
            grid=(PGROUPS,),
            in_specs=[query, query, kv, kv, kv, pl.BlockSpec((SPAN, TOK), lambda g, st: (0, 0))],
            out_specs=[flipped] * 3 + [pl.BlockSpec((GROUP, TOK), lambda g, st: (g, 0))],
        ),
        out_shape=[half] * 3 + [jax.ShapeDtypeStruct((PGROUPS * GROUP, TOK), jnp.float32)],
        cost_estimate=pl.CostEstimate(flops=8 * PQ * TOK * SPAN, bytes_accessed=6 * PQ * TOK * 2, transcendentals=2 * PQ * SPAN),
        name="forward",
    )(stage, t_query, s_query, own, nb1, nb2, bias)


def gap_body(stage_ref, s_out, t_out, recv, grad, delta, loss):
    stage = stage_ref[0].astype(jnp.float32)
    squares = jnp.zeros((8, TOK), jnp.float32)
    for h in range(PGROUPS * GROUP):
        rows = pl.ds(h * HEAD_DIM, HEAD_DIM)
        s = s_out[rows, :].astype(jnp.float32)
        t = t_out[rows, :].astype(jnp.float32)
        r = recv[rows, :].astype(jnp.float32)
        out_grad = (2.0 - stage) * (s - t) + r
        first = r - t
        sq = out_grad * out_grad + first * first
        squares = squares + jnp.sum(sq.reshape(HEAD_DIM // 8, 8, TOK), axis=0)
        half = out_grad.astype(jnp.bfloat16)
        grad[rows, :] = half
        delta[h : h + 1, :] = jnp.sum(half.astype(jnp.float32) * s, axis=0, keepdims=True)
    loss[...] = squares * stage


def gaps(stage, s_out, t_out, recv):
    heads = PGROUPS * GROUP
    whole = lambda *shape: pl.BlockSpec(shape, lambda i, st: (0,) * len(shape))
    return pl.pallas_call(
        gap_body,
        grid_spec=pltpu.PrefetchScalarGridSpec(
            num_scalar_prefetch=1,
            grid=(1,),
            in_specs=[whole(PQ, TOK)] * 3,
            out_specs=[whole(PQ, TOK), whole(heads, TOK), whole(8, TOK)],
        ),
        out_shape=[
            jax.ShapeDtypeStruct((PQ, TOK), jnp.bfloat16),
            jax.ShapeDtypeStruct((heads, TOK), jnp.float32),
            jax.ShapeDtypeStruct((8, TOK), jnp.float32),
        ],
        cost_estimate=pl.CostEstimate(flops=12 * PQ * TOK, bytes_accessed=4 * PQ * TOK * 2, transcendentals=0),
        name="gaps",
    )(stage, s_out, t_out, recv)


def backward_body(sq, own, nb1, nb2, bias, grad, delta, lse, *rest):
    dq, local, back1, back2 = rest[-4:]
    mask = jnp.concatenate([bias[...]] * PAIR, axis=1)
    keys = jnp.concatenate([nb2[0], nb1[0], own[0]], axis=0)
    values = jnp.concatenate([nb2[1], nb1[1], own[1]], axis=0)
    key_win = jnp.zeros((SPAN, HEAD_DIM), jnp.float32)
    value_win = jnp.zeros((SPAN, HEAD_DIM), jnp.float32)
    for pair in range(GROUP // PAIR):
        first = pair * PAIR
        queries = stacked(sq, pair)
        side = lambda ref, size: jnp.concatenate(
            [ref[(first + j) * size : (first + j + 1) * size, :] for j in range(PAIR)], axis=1
        )
        out_grad = side(grad, HEAD_DIM)
        scores = mm(keys, queries, NT) + mask
        prob = jnp.exp2(scores * EXP_SCALE - side(lse, 1))
        dprob = mm(values, out_grad, NN)
        dscore = (prob * (dprob - side(delta, 1))).astype(jnp.bfloat16)
        value_win = value_win + mm(prob.astype(jnp.bfloat16), out_grad, NT)
        key_win = key_win + mm(dscore, queries, NN)
        query_part = mm(dscore, keys, TN) * SCALE
        for j in range(PAIR):
            h = first + j
            dq[0, :, h * HEAD_DIM : (h + 1) * HEAD_DIM] = query_part[j * TOK : (j + 1) * TOK, :]
    key_win = key_win * SCALE
    for m, win in enumerate((key_win, value_win)):
        back2[m] = win[:TOK].astype(jnp.bfloat16)
        back1[m] = win[TOK : 2 * TOK].astype(jnp.bfloat16)
        local[m] = win[2 * TOK :]


def backward(part, s_query, own, nb1, nb2, bias, grad, delta, lse, dq):
    width = GROUP * HEAD_DIM
    query = pl.BlockSpec((1, TOK, width), lambda g: (0, 0, part * PGROUPS + g))
    kv = pl.BlockSpec((2, TOK, HEAD_DIM), lambda g: (1, 0, g))
    stat = pl.BlockSpec((GROUP, TOK), lambda g: (g, 0))
    in_specs = [query, kv, kv, kv, pl.BlockSpec((SPAN, TOK), lambda g: (0, 0))]
    in_specs += [pl.BlockSpec((width, TOK), lambda g: (g, 0)), stat, stat]
    args = [s_query, own, nb1, nb2, bias, grad, delta, lse]
    aliases = {}
    if dq is not None:
        in_specs.append(pl.BlockSpec(memory_space=pl.ANY))
        args.append(dq)
        aliases = {len(args) - 1: 0}
    pair = pl.BlockSpec((2, TOK, HEAD_DIM), lambda g: (0, 0, g))
    return pl.pallas_call(
        backward_body,
        grid=(PGROUPS,),
        in_specs=in_specs,
        out_specs=[query, pair, pair, pair],
        out_shape=[
            jax.ShapeDtypeStruct((1, TOK, HEADS * HEAD_DIM), jnp.float32),
            jax.ShapeDtypeStruct((2, TOK, PW), jnp.float32),
            jax.ShapeDtypeStruct((2, TOK, PW), jnp.bfloat16),
            jax.ShapeDtypeStruct((2, TOK, PW), jnp.bfloat16),
        ],
        input_output_aliases=aliases,
        cost_estimate=pl.CostEstimate(flops=10 * PQ * TOK * SPAN, bytes_accessed=8 * PQ * TOK, transcendentals=PQ * SPAN),
        name="backward",
    )(*args)


def finish_body(*refs):
    key_grad, value_grad = refs[-2:]
    for p in range(PARTS):
        local, ret1, ret2 = refs[3 * p : 3 * p + 3]
        cols = slice(p * PW, (p + 1) * PW)
        for m, out in enumerate((key_grad, value_grad)):
            out[0, :, cols] = local[m] + ret1[m].astype(jnp.float32) + ret2[m].astype(jnp.float32)


def finish(parts):
    shape = jax.ShapeDtypeStruct((1, TOK, KV_HEADS * HEAD_DIM), jnp.float32)
    return pl.pallas_call(finish_body, out_shape=[shape, shape], name="finish")(
        *[array for part in parts for array in part]
    )


def total_of(partial):
    value = partial
    distance = 1
    while distance < lax.axis_size("ctx"):
        value = value + rotate(value, "ctx", distance)
        distance *= 2
    value = value + rotate(value, "pipe", 1)
    return jnp.sum(value)


def per_device(t_query, t_key, t_value, s_query, s_key, s_value, segment_ids):
    pos = lax.axis_index("ctx").astype(jnp.int32).reshape(1)
    stage = lax.axis_index("pipe").astype(jnp.int32).reshape(1)
    *packs, bias = pack(pos, (t_key, t_value, s_key, s_value), segment_ids)
    near = [(rotate(block, "ctx", 1), rotate(block, "ctx", 2)) for block in packs]
    partial = jnp.zeros((8, TOK), jnp.float32)
    dq = None
    parts = []
    for part in range(PARTS):
        own, (nb1, nb2) = packs[part], near[part]
        s_out, t_out, send, lse = forward(part, stage, t_query, s_query, own, nb1, nb2, bias)
        recv = rotate(send, "pipe", 1)
        grad, delta, squares = gaps(stage, s_out, t_out, recv)
        partial = partial + squares
        dq, local, back1, back2 = backward(
            part, s_query, own, nb1, nb2, bias, grad, delta, lse, dq
        )
        parts.append((local, rotate(back1, "ctx", -1), rotate(back2, "ctx", -2)))
    sections, tokens = lax.axis_size("pipe"), lax.axis_size("ctx") * TOK
    loss = total_of(partial) / float(sections * tokens * HEADS * HEAD_DIM)
    key_grad, value_grad = finish(parts)
    return (loss, dq, key_grad, value_grad)


def solution(mesh):
    placed = P("pipe", "ctx", None)
    return jax.shard_map(
        per_device,
        mesh=mesh,
        in_specs=(placed,) * 6 + (P(),),
        out_specs=(P(), placed, placed, placed),
        check_vma=False,
    )
```

```python
import functools
import jax
import jax.numpy as jnp
from jax import lax
from jax.experimental import pallas as pl
from jax.experimental.pallas import tpu as pltpu
from jax.sharding import PartitionSpec as P

REACH = 2
HEADS = 32
KV_HEADS = 4
HEAD_DIM = 128
GROUP = HEADS // KV_HEADS
TOK = 128
SPAN = (REACH + 1) * TOK
SPLIT = (1, 1, 2)
PARTS = len(SPLIT)
OFFSET = tuple(sum(SPLIT[:p]) for p in range(PARTS))
PAIR = 2

NEG_FILL = -1e30
SCALE = HEAD_DIM ** (-0.5)
LOG2E = 1.4426950408889634
EXP_SCALE = SCALE * LOG2E
NT = (((1,), (1,)), ((), ()))
NN = (((1,), (0,)), ((), ()))
TN = (((0,), (0,)), ((), ()))


def mm(a, b, dims):
    return lax.dot_general(a, b, dims, preferred_element_type=jnp.float32)


def rotate(block, axis, distance):
    count = lax.axis_size(axis)
    return lax.ppermute(block, axis, [(i, (i + distance) % count) for i in range(count)])


def in_hbm(array):
    return pltpu.with_memory_space_constraint(array, pltpu.HBM)


def pack_body(pos_ref, tk, tv, sk, sv, seg0, seg1, seg2, *outs):
    packs, (bias, first_rows, first_cols) = outs[:PARTS], outs[PARTS:]
    for p in range(PARTS):
        for m, src in enumerate((tk, tv, sk, sv)):
            packs[p][m] = src[0, :, OFFSET[p] * HEAD_DIM : (OFFSET[p] + SPLIT[p]) * HEAD_DIM]
    square = lambda seg: jnp.broadcast_to(seg[0].astype(jnp.float32), (TOK, TOK))
    queries = square(seg0)
    keys0, keys1, keys2 = queries.T, square(seg1).T, square(seg2).T
    first = jnp.broadcast_to(keys0[0:1, :], (TOK, TOK))
    in_first = queries == first
    key_in_first = keys0 == first
    row = lax.broadcasted_iota(jnp.int32, (TOK, TOK), 0)
    col = lax.broadcasted_iota(jnp.int32, (TOK, TOK), 1)
    own_ok = (keys0 == queries) & (row <= col)
    near_ok = in_first & (keys1 == queries)
    far_ok = in_first & (keys2 == queries) & jnp.logical_not(key_in_first)
    bias[:TOK, :] = jnp.where(near_ok, 0.0, NEG_FILL)
    bias[TOK:, :] = jnp.where(own_ok | far_ok, 0.0, NEG_FILL)
    first_rows[...] = jnp.where(key_in_first, 1.0, 0.0)
    first_cols[...] = jnp.where(in_first, 1.0, 0.0)


def pack(pos, blocks, segment_ids):
    count = segment_ids.shape[0] // TOK
    seg = segment_ids.reshape(count, 1, TOK)
    kv = pl.BlockSpec((1, TOK, KV_HEADS * HEAD_DIM), lambda i, pos: (0, 0, 0))
    segs = [
        pl.BlockSpec((1, 1, TOK), lambda i, pos, d=d: (lax.rem(pos[0] + count - d, count), 0, 0))
        for d in range(REACH + 1)
    ]
    whole = lambda *shape: pl.BlockSpec(shape, lambda i, pos: (0,) * len(shape))
    flat = jax.ShapeDtypeStruct((TOK, TOK), jnp.float32)
    return pl.pallas_call(
        pack_body,
        grid_spec=pltpu.PrefetchScalarGridSpec(
            num_scalar_prefetch=1,
            grid=(1,),
            in_specs=[kv] * 4 + segs,
            out_specs=[whole(4, TOK, n * HEAD_DIM) for n in SPLIT] + [whole(2 * TOK, TOK)] + [whole(TOK, TOK)] * 2,
        ),
        out_shape=[jax.ShapeDtypeStruct((4, TOK, n * HEAD_DIM), jnp.bfloat16) for n in SPLIT]
        + [jax.ShapeDtypeStruct((2 * TOK, TOK), jnp.float32), flat, flat],
        name="pack",
    )(pos, *blocks, seg, seg, seg)


def window(own, nb1, nb2, rows):
    mixed = own * rows + nb2 * (1 - rows)
    upper = jnp.concatenate([nb1, jnp.zeros_like(nb1)], axis=1)
    return jnp.concatenate([upper, jnp.concatenate([mixed, own], axis=1)], axis=0)


def query_pair(q_ref, pair, rows):
    parts = []
    for j in range(PAIR):
        h = pair * PAIR + j
        q = q_ref[0, :, h * HEAD_DIM : (h + 1) * HEAD_DIM]
        early = q * rows
        parts.append(jnp.concatenate([early, q - early], axis=1))
    return jnp.concatenate(parts, axis=0)


def forward_body(stage_ref, tq, sq, own, nb1, nb2, bias, frow, fcol, s_out, t_out, send, lse):
    ahead = stage_ref[0].astype(jnp.float32) + 1.0
    rows = frow[...].astype(jnp.bfloat16)
    early = fcol[0:1, :] > 0.5
    models = []
    for base in (0, 2):
        keys = window(own[base], nb1[base], nb2[base], rows)
        v0, v1, v2 = own[base + 1], nb1[base + 1], nb2[base + 1]
        mixed = (v0 * rows + v2 * (1 - rows)).T
        values = jnp.concatenate(
            [
                jnp.concatenate([v1.T, mixed], axis=1),
                jnp.concatenate([jnp.zeros((HEAD_DIM, TOK), jnp.bfloat16), v0.T], axis=1),
            ],
            axis=0,
        )
        models.append((keys, values))
    items = [(pair, model) for pair in range(GROUP // PAIR) for model in (0, 1)]

    def score(item):
        pair, model = item
        return mm(models[model][0], query_pair((tq, sq)[model], pair, rows), NT)

    def soften(scores):
        halves, inverses, levels = [], [], []
        for j in range(PAIR):
            s = scores[:, j * TOK : (j + 1) * TOK] + bias[...]
            peak = jnp.max(s, axis=0, keepdims=True)
            expo = jnp.exp2((s - peak) * EXP_SCALE)
            total = jnp.sum(expo, axis=0, keepdims=True)
            halves.append(expo.astype(jnp.bfloat16))
            inverses.append(1.0 / total)
            levels.append(peak * EXP_SCALE + jnp.log2(total))
        return jnp.concatenate(halves, axis=1), inverses, levels

    def mix(item, weights, inverses):
        both = mm(models[item[1]][1], weights, NN)
        outs = []
        for j in range(PAIR):
            cols = slice(j * TOK, (j + 1) * TOK)
            picked = jnp.where(early, both[:HEAD_DIM, cols], both[HEAD_DIM:, cols])
            outs.append((picked * inverses[j]).astype(jnp.bfloat16))
        return outs

    ready = score(items[0])
    teacher = None
    for n, item in enumerate(items):
        following = score(items[n + 1]) if n + 1 < len(items) else None
        weights, inverses, levels = soften(ready)
        outs = mix(item, weights, inverses)
        ready = following
        if item[1] == 0:
            teacher = outs
            continue
        for j in range(PAIR):
            h = item[0] * PAIR + j
            at = pl.ds(h * HEAD_DIM, HEAD_DIM)
            s_out[at, :] = outs[j]
            t_out[at, :] = teacher[j]
            send[at, :] = (
                outs[j].astype(jnp.float32) - ahead * teacher[j].astype(jnp.float32)
            ).astype(jnp.bfloat16)
            lse[h : h + 1, :] = levels[j]


def forward(part, stage, t_query, s_query, own, nb1, nb2, masks):
    width = GROUP * HEAD_DIM
    groups = SPLIT[part]
    total = groups * width
    query = pl.BlockSpec((1, TOK, width), lambda g, st: (0, 0, OFFSET[part] + g))
    kv = pl.BlockSpec((4, TOK, HEAD_DIM), lambda g, st: (0, 0, g))
    flipped = pl.BlockSpec((width, TOK), lambda g, st: (g, 0))
    half = jax.ShapeDtypeStruct((total, TOK), jnp.bfloat16)
    fixed = [pl.BlockSpec(m.shape, lambda g, st: (0, 0)) for m in masks]
    return pl.pallas_call(
        forward_body,
        grid_spec=pltpu.PrefetchScalarGridSpec(
            num_scalar_prefetch=1,
            grid=(groups,),
            in_specs=[query, query, kv, kv, kv] + fixed,
            out_specs=[flipped] * 3 + [pl.BlockSpec((GROUP, TOK), lambda g, st: (g, 0))],
        ),
        out_shape=[half] * 3 + [jax.ShapeDtypeStruct((groups * GROUP, TOK), jnp.float32)],
        cost_estimate=pl.CostEstimate(flops=8 * total * TOK * SPAN, bytes_accessed=6 * total * TOK * 2, transcendentals=2 * total * SPAN),
        name="forward",
    )(stage, t_query, s_query, own, nb1, nb2, *masks)


def backward_body(several, chained, stage_ref, sq, own, nb1, nb2, bias, frow, fcol, s_out, t_out, recv, lse, *rest):
    dq, local, back1, back2, loss, all_query, all_grad, all_prob, all_score = rest[-9:]
    stage = stage_ref[0].astype(jnp.float32)
    rows = frow[...].astype(jnp.bfloat16)
    cols_mask = fcol[...].astype(jnp.bfloat16)
    keys = window(own[0], nb1[0], nb2[0], rows)
    values = window(own[1], nb1[1], nb2[1], rows)
    width = PAIR * TOK
    squares = [jnp.zeros((8, TOK), jnp.float32)]

    def out_grad_of(h):
        at = slice(h * HEAD_DIM, (h + 1) * HEAD_DIM)
        s = s_out[at, :].astype(jnp.float32)
        t = t_out[at, :].astype(jnp.float32)
        r = recv[at, :].astype(jnp.float32)
        grad = (2.0 - stage) * (s - t) + r
        first = r - t
        both = grad * grad + first * first
        squares[0] = squares[0] + jnp.sum(both.reshape(HEAD_DIM // 8, 8, TOK), axis=0)
        half = grad.astype(jnp.bfloat16)
        return half, jnp.sum(half.astype(jnp.float32) * s, axis=0, keepdims=True)

    def start(pair):
        at = slice(pair * width, (pair + 1) * width)
        queries = query_pair(sq, pair, rows)
        all_query[at, :] = queries
        stacked, deltas = [], []
        for j in range(PAIR):
            g, delta = out_grad_of(pair * PAIR + j)
            early = g * cols_mask
            stacked.append(jnp.concatenate([early, g - early], axis=0))
            deltas.append(delta)
        out_grad = jnp.concatenate(stacked, axis=1)
        all_grad[:, at] = out_grad
        return mm(keys, queries, NT), mm(values, out_grad, NN), deltas

    ready = start(0)
    for pair in range(GROUP // PAIR):
        scores, dprob, deltas = ready
        if pair + 1 < GROUP // PAIR:
            ready = start(pair + 1)
        for j in range(PAIR):
            h = pair * PAIR + j
            part = slice(j * TOK, (j + 1) * TOK)
            at = slice(h * TOK, (h + 1) * TOK)
            prob = jnp.exp2((scores[:, part] + bias[...]) * EXP_SCALE - lse[h : h + 1, :])
            dscore = prob * (dprob[:, part] - deltas[j])
            all_prob[:, at] = prob.astype(jnp.bfloat16)
            all_score[:, at] = dscore.astype(jnp.bfloat16)
        at = slice(pair * width, (pair + 1) * width)
        query_part = mm(all_score[:, at], keys, TN)
        for j in range(PAIR):
            h = pair * PAIR + j
            both = query_part[j * TOK : (j + 1) * TOK, :]
            picked = jnp.where(frow[...] > 0.5, both[:, :HEAD_DIM], both[:, HEAD_DIM:])
            dq[0, :, h * HEAD_DIM : (h + 1) * HEAD_DIM] = picked * SCALE
    key_win = mm(all_score[...], all_query[...], NN) * SCALE
    value_win = mm(all_prob[...], all_grad[...], NT)
    for m, win in enumerate((key_win, value_win)):
        back1[m] = win[:TOK, :HEAD_DIM].astype(jnp.bfloat16)
        mixed = win[TOK:, :HEAD_DIM]
        kept = mixed * frow[...]
        back2[m] = (mixed - kept).astype(jnp.bfloat16)
        local[m] = win[TOK:, HEAD_DIM:] + kept
    total = jnp.sum(squares[0], axis=0, keepdims=True) * stage
    step = pl.program_id(0)
    before = rest[0][0:1, :] if chained else jnp.zeros((1, TOK), jnp.float32)
    if several:
        before = jnp.where(step == 0, before, loss[0:1, :])
    loss[...] = jnp.broadcast_to(total + before, loss.shape)


def backward(part, stage, s_query, own, nb1, nb2, masks, outs, recv, lse, carried, senders):
    width = GROUP * HEAD_DIM
    groups = SPLIT[part]
    total = groups * width
    last = part == PARTS - 1
    flat = senders if last else 8
    query = pl.BlockSpec((1, TOK, width), lambda g, st: (0, 0, OFFSET[part] + g))
    kv = pl.BlockSpec((2, TOK, HEAD_DIM), lambda g, st: (1, 0, g))
    flipped = pl.BlockSpec((width, TOK), lambda g, st: (g, 0))
    fixed = lambda shape: pl.BlockSpec(shape, lambda g, st: (0,) * len(shape))
    in_specs = [query, kv, kv, kv] + [fixed(m.shape) for m in masks]
    in_specs += [flipped] * 3 + [pl.BlockSpec((GROUP, TOK), lambda g, st: (g, 0))]
    args = [stage, s_query, own, nb1, nb2, *masks, *outs, recv, lse]
    aliases = {}
    if carried is not None:
        *buffers, squares = carried
        in_specs.append(fixed(squares.shape))
        args.append(squares)
        for n, buffer in enumerate(buffers):
            aliases[len(args)] = n
            in_specs.append(pl.BlockSpec(memory_space=pl.ANY))
            args.append(buffer)
    pair = pl.BlockSpec((2, TOK, HEAD_DIM), lambda g, st: (0, 0, OFFSET[part] + g))
    wide = (2, TOK, KV_HEADS * HEAD_DIM)
    return pl.pallas_call(
        functools.partial(backward_body, groups > 1, carried is not None),
        grid_spec=pltpu.PrefetchScalarGridSpec(
            num_scalar_prefetch=1,
            grid=(groups,),
            in_specs=in_specs,
            out_specs=[query, pair, pair, pair, fixed((flat, TOK))],
            scratch_shapes=[
                pltpu.VMEM((GROUP * TOK, 2 * HEAD_DIM), jnp.bfloat16),
                pltpu.VMEM((2 * HEAD_DIM, GROUP * TOK), jnp.bfloat16),
                pltpu.VMEM((2 * TOK, GROUP * TOK), jnp.bfloat16),
                pltpu.VMEM((2 * TOK, GROUP * TOK), jnp.bfloat16),
            ],
        ),
        out_shape=[
            jax.ShapeDtypeStruct((1, TOK, HEADS * HEAD_DIM), jnp.float32),
            jax.ShapeDtypeStruct(wide, jnp.float32),
            jax.ShapeDtypeStruct(wide, jnp.bfloat16),
            jax.ShapeDtypeStruct(wide, jnp.bfloat16),
            jax.ShapeDtypeStruct((flat, TOK), jnp.float32),
        ],
        input_output_aliases=aliases,
        cost_estimate=pl.CostEstimate(flops=10 * total * TOK * SPAN, bytes_accessed=12 * total * TOK, transcendentals=total * SPAN),
        name="backward",
    )(*args)


def finish_body(local, ret1, ret2, squares, loss, key_grad, value_grad):
    for m, out in enumerate((key_grad, value_grad)):
        out[0] = local[m] + ret1[m].astype(jnp.float32) + ret2[m].astype(jnp.float32)
    count = squares.shape[0] * TOK * HEADS * HEAD_DIM
    rows = jnp.sum(squares[...], axis=0, keepdims=True)
    loss[...] = jnp.sum(rows, axis=1, keepdims=True) * (1.0 / count)


def finish(local, ret1, ret2, squares):
    shape = jax.ShapeDtypeStruct((1, TOK, KV_HEADS * HEAD_DIM), jnp.float32)
    return pl.pallas_call(
        finish_body,
        out_shape=[jax.ShapeDtypeStruct((1, 1), jnp.float32), shape, shape],
        name="finish",
    )(local, ret1, ret2, squares)


def per_device(t_query, t_key, t_value, s_query, s_key, s_value, segment_ids):
    pos = lax.axis_index("ctx").astype(jnp.int32).reshape(1)
    stage = lax.axis_index("pipe").astype(jnp.int32).reshape(1)
    senders = lax.axis_size("pipe") * lax.axis_size("ctx")
    packed = pack(pos, (t_key, t_value, s_key, s_value), segment_ids)
    packs, masks = packed[:PARTS], packed[PARTS:]
    near = []
    for block in packs:
        pair = []
        for d in (1, 2):
            pair.append(in_hbm(rotate(block, "ctx", d)))
        near.append(pair)
    carried = None
    waiting = []

    def close(carried):
        part, outs, recv, lse = waiting.pop(0)
        own, (nb1, nb2) = packs[part], near[part]
        return backward(
            part, stage, s_query, own, nb1, nb2, masks, outs, recv, lse, carried, senders
        )

    for part in range(PARTS):
        own, (nb1, nb2) = packs[part], near[part]
        mark = stage
        if carried is not None:
            mark, held = lax.optimization_barrier((stage, carried[-1]))
            carried = (*carried[:-1], held)
        s_out, t_out, send, lse = forward(part, mark, t_query, s_query, own, nb1, nb2, masks)
        waiting.append((part, (s_out, t_out), in_hbm(rotate(send, "pipe", 1)), lse))
        carried = close(carried)
    dq, local, back1, back2, squares = carried
    ret1, ret2 = in_hbm(rotate(back1, "ctx", -1)), in_hbm(rotate(back2, "ctx", -2))
    gathered = lax.all_to_all(squares, ("ctx", "pipe"), 0, 0, tiled=True)
    loss, key_grad, value_grad = finish(local, ret1, ret2, gathered)
    return (loss.reshape(()), dq, key_grad, value_grad)


def solution(mesh):
    placed = P("pipe", "ctx", None)
    return jax.shard_map(
        per_device,
        mesh=mesh,
        in_specs=(placed,) * 6 + (P(),),
        out_specs=(P(), placed, placed, placed),
        check_vma=False,
    )
```

```python
import functools
import jax
import jax.numpy as jnp
from jax import lax
from jax.experimental import pallas as pl
from jax.experimental.pallas import tpu as pltpu
from jax.sharding import PartitionSpec as P

REACH = 2
HEADS = 32
KV_HEADS = 4
HEAD_DIM = 128
GROUP = HEADS // KV_HEADS
TOK = 128
SPAN = (REACH + 1) * TOK
SPLIT = (1, 1, 2)
PARTS = len(SPLIT)
OFFSET = tuple(sum(SPLIT[:p]) for p in range(PARTS))
PAIR = 2
VMEM_LIMIT = 16 << 20
X_CHIPS = 4
RELAYED = (2,)

NEG_FILL = -1e30
SCALE = HEAD_DIM ** (-0.5)
LOG2E = 1.4426950408889634
EXP_SCALE = SCALE * LOG2E
NT = (((1,), (1,)), ((), ()))
NN = (((1,), (0,)), ((), ()))
TN = (((0,), (0,)), ((), ()))


def mm(a, b, dims):
    return lax.dot_general(a, b, dims, preferred_element_type=jnp.float32)


def rotate(block, axis, distance):
    count = lax.axis_size(axis)
    return lax.ppermute(block, axis, [(i, (i + distance) % count) for i in range(count)])


def in_hbm(array):
    return pltpu.with_memory_space_constraint(array, pltpu.HBM)


def pack_body(pos_ref, tk, tv, sk, sv, seg0, seg1, seg2, *outs):
    packs, (bias, first_rows, first_cols) = outs[:PARTS], outs[PARTS:]
    for p in range(PARTS):
        for m, src in enumerate((tk, tv, sk, sv)):
            packs[p][m] = src[0, :, OFFSET[p] * HEAD_DIM : (OFFSET[p] + SPLIT[p]) * HEAD_DIM]
    square = lambda seg: jnp.broadcast_to(seg[0].astype(jnp.float32), (TOK, TOK))
    queries = square(seg0)
    keys0, keys1, keys2 = queries.T, square(seg1).T, square(seg2).T
    first = jnp.broadcast_to(keys0[0:1, :], (TOK, TOK))
    in_first = queries == first
    key_in_first = keys0 == first
    row = lax.broadcasted_iota(jnp.int32, (TOK, TOK), 0)
    col = lax.broadcasted_iota(jnp.int32, (TOK, TOK), 1)
    own_ok = (keys0 == queries) & (row <= col)
    near_ok = in_first & (keys1 == queries)
    far_ok = in_first & (keys2 == queries) & jnp.logical_not(key_in_first)
    bias[:TOK, :] = jnp.where(near_ok, 0.0, NEG_FILL)
    bias[TOK:, :] = jnp.where(own_ok | far_ok, 0.0, NEG_FILL)
    first_rows[...] = jnp.where(key_in_first, 1.0, 0.0)
    first_cols[...] = jnp.where(in_first, 1.0, 0.0)


def pack(pos, blocks, segment_ids):
    count = segment_ids.shape[0] // TOK
    seg = segment_ids.reshape(count, 1, TOK)
    kv = pl.BlockSpec((1, TOK, KV_HEADS * HEAD_DIM), lambda i, pos: (0, 0, 0))
    segs = [
        pl.BlockSpec((1, 1, TOK), lambda i, pos, d=d: (lax.rem(pos[0] + count - d, count), 0, 0))
        for d in range(REACH + 1)
    ]
    whole = lambda *shape: pl.BlockSpec(shape, lambda i, pos: (0,) * len(shape))
    flat = jax.ShapeDtypeStruct((TOK, TOK), jnp.float32)
    return pl.pallas_call(
        pack_body,
        grid_spec=pltpu.PrefetchScalarGridSpec(
            num_scalar_prefetch=1,
            grid=(1,),
            in_specs=[kv] * 4 + segs,
            out_specs=[whole(4, TOK, n * HEAD_DIM) for n in SPLIT] + [whole(2 * TOK, TOK)] + [whole(TOK, TOK)] * 2,
        ),
        out_shape=[jax.ShapeDtypeStruct((4, TOK, n * HEAD_DIM), jnp.bfloat16) for n in SPLIT]
        + [jax.ShapeDtypeStruct((2 * TOK, TOK), jnp.float32), flat, flat],
        compiler_params=pltpu.CompilerParams(vmem_limit_bytes=VMEM_LIMIT),
        name="pack",
    )(pos, *[in_hbm(b) for b in blocks], *[in_hbm(seg)] * 3)


def window(own, nb1, nb2, rows):
    mixed = own * rows + nb2 * (1 - rows)
    upper = jnp.concatenate([nb1, jnp.zeros_like(nb1)], axis=1)
    return jnp.concatenate([upper, jnp.concatenate([mixed, own], axis=1)], axis=0)


def query_pair(q_ref, pair, rows):
    parts = []
    for j in range(PAIR):
        h = pair * PAIR + j
        q = q_ref[0, :, h * HEAD_DIM : (h + 1) * HEAD_DIM]
        early = q * rows
        parts.append(jnp.concatenate([early, q - early], axis=1))
    return jnp.concatenate(parts, axis=0)


def forward_body(stage_ref, tq, sq, own, nb1, nb2, bias, frow, fcol, s_out, t_out, send, lse):
    ahead = stage_ref[0].astype(jnp.float32) + 1.0
    rows = frow[...].astype(jnp.bfloat16)
    early = fcol[0:1, :] > 0.5
    models = []
    for base in (0, 2):
        keys = window(own[base], nb1[base], nb2[base], rows)
        v0, v1, v2 = own[base + 1], nb1[base + 1], nb2[base + 1]
        mixed = (v0 * rows + v2 * (1 - rows)).T
        values = jnp.concatenate(
            [
                jnp.concatenate([v1.T, mixed], axis=1),
                jnp.concatenate([jnp.zeros((HEAD_DIM, TOK), jnp.bfloat16), v0.T], axis=1),
            ],
            axis=0,
        )
        models.append((keys, values))
    items = [(pair, model) for pair in range(GROUP // PAIR) for model in (0, 1)]

    def score(item):
        pair, model = item
        return mm(models[model][0], query_pair((tq, sq)[model], pair, rows), NT)

    def soften(scores):
        halves, inverses, levels = [], [], []
        for j in range(PAIR):
            s = scores[:, j * TOK : (j + 1) * TOK] + bias[...]
            peak = jnp.max(s, axis=0, keepdims=True)
            expo = jnp.exp2((s - peak) * EXP_SCALE)
            total = jnp.sum(expo, axis=0, keepdims=True)
            halves.append(expo.astype(jnp.bfloat16))
            inverses.append(1.0 / total)
            levels.append(peak * EXP_SCALE + jnp.log2(total))
        return jnp.concatenate(halves, axis=1), inverses, levels

    def mix(item, weights, inverses):
        both = mm(models[item[1]][1], weights, NN)
        outs = []
        for j in range(PAIR):
            cols = slice(j * TOK, (j + 1) * TOK)
            picked = jnp.where(early, both[:HEAD_DIM, cols], both[HEAD_DIM:, cols])
            outs.append((picked * inverses[j]).astype(jnp.bfloat16))
        return outs

    ready = score(items[0])
    teacher = None
    for n, item in enumerate(items):
        following = score(items[n + 1]) if n + 1 < len(items) else None
        weights, inverses, levels = soften(ready)
        outs = mix(item, weights, inverses)
        ready = following
        if item[1] == 0:
            teacher = outs
            continue
        for j in range(PAIR):
            h = item[0] * PAIR + j
            at = pl.ds(h * HEAD_DIM, HEAD_DIM)
            s_out[at, :] = outs[j]
            t_out[at, :] = teacher[j]
            send[at, :] = (
                outs[j].astype(jnp.float32) - ahead * teacher[j].astype(jnp.float32)
            ).astype(jnp.bfloat16)
            lse[h : h + 1, :] = levels[j]


def forward(part, stage, t_query, s_query, own, nb1, nb2, masks):
    width = GROUP * HEAD_DIM
    groups = SPLIT[part]
    total = groups * width
    query = pl.BlockSpec((1, TOK, width), lambda g, st: (0, 0, OFFSET[part] + g))
    kv = pl.BlockSpec((4, TOK, HEAD_DIM), lambda g, st: (0, 0, g))
    flipped = pl.BlockSpec((width, TOK), lambda g, st: (g, 0))
    half = jax.ShapeDtypeStruct((total, TOK), jnp.bfloat16)
    fixed = [pl.BlockSpec(m.shape, lambda g, st: (0, 0)) for m in masks]
    return pl.pallas_call(
        forward_body,
        grid_spec=pltpu.PrefetchScalarGridSpec(
            num_scalar_prefetch=1,
            grid=(groups,),
            in_specs=[query, query, kv, kv, kv] + fixed,
            out_specs=[flipped] * 3 + [pl.BlockSpec((GROUP, TOK), lambda g, st: (g, 0))],
        ),
        out_shape=[half] * 3 + [jax.ShapeDtypeStruct((groups * GROUP, TOK), jnp.float32)],
        cost_estimate=pl.CostEstimate(flops=8 * total * TOK * SPAN, bytes_accessed=6 * total * TOK * 2, transcendentals=2 * total * SPAN),
        compiler_params=pltpu.CompilerParams(vmem_limit_bytes=VMEM_LIMIT),
        name="forward",
    )(stage, in_hbm(t_query), in_hbm(s_query), own, nb1, nb2, *masks)


def backward_body(several, chained, stage_ref, sq, own, nb1, nb2, bias, frow, fcol, s_out, t_out, recv, lse, *rest):
    dq, local, back1, back2, loss, all_query, all_grad, all_prob, all_score = rest[-9:]
    stage = stage_ref[0].astype(jnp.float32)
    rows = frow[...].astype(jnp.bfloat16)
    cols_mask = fcol[...].astype(jnp.bfloat16)
    keys = window(own[0], nb1[0], nb2[0], rows)
    values = window(own[1], nb1[1], nb2[1], rows)
    width = PAIR * TOK
    squares = [jnp.zeros((8, TOK), jnp.float32)]

    def out_grad_of(h):
        at = slice(h * HEAD_DIM, (h + 1) * HEAD_DIM)
        s = s_out[at, :].astype(jnp.float32)
        t = t_out[at, :].astype(jnp.float32)
        r = recv[at, :].astype(jnp.float32)
        grad = (2.0 - stage) * (s - t) + r
        first = r - t
        both = grad * grad + first * first
        squares[0] = squares[0] + jnp.sum(both.reshape(HEAD_DIM // 8, 8, TOK), axis=0)
        half = grad.astype(jnp.bfloat16)
        return half, jnp.sum(half.astype(jnp.float32) * s, axis=0, keepdims=True)

    def start(pair):
        at = slice(pair * width, (pair + 1) * width)
        queries = query_pair(sq, pair, rows)
        all_query[at, :] = queries
        stacked, deltas = [], []
        for j in range(PAIR):
            g, delta = out_grad_of(pair * PAIR + j)
            early = g * cols_mask
            stacked.append(jnp.concatenate([early, g - early], axis=0))
            deltas.append(delta)
        out_grad = jnp.concatenate(stacked, axis=1)
        all_grad[:, at] = out_grad
        return mm(keys, queries, NT), mm(values, out_grad, NN), deltas

    ready = start(0)
    for pair in range(GROUP // PAIR):
        scores, dprob, deltas = ready
        if pair + 1 < GROUP // PAIR:
            ready = start(pair + 1)
        for j in range(PAIR):
            h = pair * PAIR + j
            part = slice(j * TOK, (j + 1) * TOK)
            at = slice(h * TOK, (h + 1) * TOK)
            prob = jnp.exp2((scores[:, part] + bias[...]) * EXP_SCALE - lse[h : h + 1, :])
            dscore = prob * (dprob[:, part] - deltas[j])
            all_prob[:, at] = prob.astype(jnp.bfloat16)
            all_score[:, at] = dscore.astype(jnp.bfloat16)
        at = slice(pair * width, (pair + 1) * width)
        query_part = mm(all_score[:, at], keys, TN)
        for j in range(PAIR):
            h = pair * PAIR + j
            both = query_part[j * TOK : (j + 1) * TOK, :]
            picked = jnp.where(frow[...] > 0.5, both[:, :HEAD_DIM], both[:, HEAD_DIM:])
            dq[0, :, h * HEAD_DIM : (h + 1) * HEAD_DIM] = picked * SCALE
    key_win = mm(all_score[...], all_query[...], NN) * SCALE
    value_win = mm(all_prob[...], all_grad[...], NT)
    for m, win in enumerate((key_win, value_win)):
        back1[m] = win[:TOK, :HEAD_DIM].astype(jnp.bfloat16)
        mixed = win[TOK:, :HEAD_DIM]
        kept = mixed * frow[...]
        back2[m] = (mixed - kept).astype(jnp.bfloat16)
        local[m] = win[TOK:, HEAD_DIM:] + kept
    total = jnp.sum(squares[0], axis=0, keepdims=True) * stage
    step = pl.program_id(0)
    before = rest[0][0:1, :] if chained else jnp.zeros((1, TOK), jnp.float32)
    if several:
        before = jnp.where(step == 0, before, loss[0:1, :])
    loss[...] = jnp.broadcast_to(total + before, loss.shape)


def backward(part, stage, s_query, own, nb1, nb2, masks, outs, recv, lse, carried, senders):
    width = GROUP * HEAD_DIM
    groups = SPLIT[part]
    total = groups * width
    last = part == PARTS - 1
    flat = senders if last else 8
    query = pl.BlockSpec((1, TOK, width), lambda g, st: (0, 0, OFFSET[part] + g))
    kv = pl.BlockSpec((2, TOK, HEAD_DIM), lambda g, st: (1, 0, g))
    flipped = pl.BlockSpec((width, TOK), lambda g, st: (g, 0))
    fixed = lambda shape: pl.BlockSpec(shape, lambda g, st: (0,) * len(shape))
    in_specs = [query, kv, kv, kv] + [fixed(m.shape) for m in masks]
    in_specs += [flipped] * 3 + [pl.BlockSpec((GROUP, TOK), lambda g, st: (g, 0))]
    args = [stage, in_hbm(s_query), own, nb1, nb2, *masks, *outs, recv, lse]
    aliases = {}
    if carried is not None:
        *buffers, squares = carried
        in_specs.append(fixed(squares.shape))
        args.append(squares)
        for n, buffer in enumerate(buffers):
            aliases[len(args)] = n
            in_specs.append(pl.BlockSpec(memory_space=pl.ANY))
            args.append(buffer)
    pair = pl.BlockSpec((2, TOK, HEAD_DIM), lambda g, st: (0, 0, OFFSET[part] + g))
    wide = (2, TOK, KV_HEADS * HEAD_DIM)
    return pl.pallas_call(
        functools.partial(backward_body, groups > 1, carried is not None),
        grid_spec=pltpu.PrefetchScalarGridSpec(
            num_scalar_prefetch=1,
            grid=(groups,),
            in_specs=in_specs,
            out_specs=[query, pair, pair, pair, fixed((flat, TOK))],
            scratch_shapes=[
                pltpu.VMEM((GROUP * TOK, 2 * HEAD_DIM), jnp.bfloat16),
                pltpu.VMEM((2 * HEAD_DIM, GROUP * TOK), jnp.bfloat16),
                pltpu.VMEM((2 * TOK, GROUP * TOK), jnp.bfloat16),
                pltpu.VMEM((2 * TOK, GROUP * TOK), jnp.bfloat16),
            ],
        ),
        out_shape=[
            jax.ShapeDtypeStruct((1, TOK, HEADS * HEAD_DIM), jnp.float32),
            jax.ShapeDtypeStruct(wide, jnp.float32),
            jax.ShapeDtypeStruct(wide, jnp.bfloat16),
            jax.ShapeDtypeStruct(wide, jnp.bfloat16),
            jax.ShapeDtypeStruct((flat, TOK), jnp.float32),
        ],
        input_output_aliases=aliases,
        cost_estimate=pl.CostEstimate(flops=10 * total * TOK * SPAN, bytes_accessed=12 * total * TOK, transcendentals=total * SPAN),
        compiler_params=pltpu.CompilerParams(vmem_limit_bytes=VMEM_LIMIT),
        name="backward",
    )(*args)


def finish_body(local, ret1, ret2, squares, loss, key_grad, value_grad):
    for m, out in enumerate((key_grad, value_grad)):
        out[0] = local[m] + ret1[m].astype(jnp.float32) + ret2[m].astype(jnp.float32)
    count = squares.shape[0] * TOK * HEADS * HEAD_DIM
    rows = jnp.sum(squares[...], axis=0, keepdims=True)
    loss[...] = jnp.sum(rows, axis=1, keepdims=True) * (1.0 / count)


def finish(local, ret1, ret2, squares):
    shape = jax.ShapeDtypeStruct((1, TOK, KV_HEADS * HEAD_DIM), jnp.float32)
    return pl.pallas_call(
        finish_body,
        out_shape=[jax.ShapeDtypeStruct((1, 1), jnp.float32), shape, shape],
        compiler_params=pltpu.CompilerParams(vmem_limit_bytes=VMEM_LIMIT),
        name="finish",
    )(local, ret1, ret2, squares)


def relay_routes(count):
    first, second = [], []
    for i in range(count):
        x = i % X_CHIPS
        first.append((i, i - 1 if x else i + X_CHIPS - 1))
        second.append((i, i - 1 if x == X_CHIPS - 1 else (i + X_CHIPS - 1) % count))
    return first, second


def per_device(t_query, t_key, t_value, s_query, s_key, s_value, segment_ids):
    pos = lax.axis_index("ctx").astype(jnp.int32).reshape(1)
    stage = lax.axis_index("pipe").astype(jnp.int32).reshape(1)
    senders = lax.axis_size("pipe") * lax.axis_size("ctx")
    packed = pack(pos, (t_key, t_value, s_key, s_value), segment_ids)
    packs, masks = packed[:PARTS], packed[PARTS:]
    near = []
    for part, block in enumerate(packs):
        nb1 = rotate(block, "ctx", 1)
        if part in RELAYED:
            first, second = relay_routes(lax.axis_size("ctx"))
            nb2 = lax.ppermute(block, "ctx", first)
            nb2 = lax.ppermute(nb2, "ctx", second)
        else:
            nb2 = rotate(block, "ctx", 2)
        near.append((nb1, nb2))
    carried = None
    waiting = []

    def close(carried):
        part, outs, recv, lse = waiting.pop(0)
        own, (nb1, nb2) = packs[part], near[part]
        return backward(
            part, stage, s_query, own, nb1, nb2, masks, outs, recv, lse, carried, senders
        )

    for part in range(PARTS):
        own, (nb1, nb2) = packs[part], near[part]
        mark = stage
        if carried is not None:
            mark, held = lax.optimization_barrier((stage, carried[-1]))
            carried = (*carried[:-1], held)
        s_out, t_out, send, lse = forward(part, mark, t_query, s_query, own, nb1, nb2, masks)
        waiting.append((part, (s_out, t_out), (rotate(send, "pipe", 1)), lse))
        carried = close(carried)
    dq, local, back1, back2, squares = carried
    ret1, ret2 = (rotate(back1, "ctx", -1)), (rotate(back2, "ctx", -2))
    gathered = lax.all_to_all(squares, ("ctx", "pipe"), 0, 0, tiled=True)
    loss, key_grad, value_grad = finish(local, ret1, ret2, gathered)
    return (loss.reshape(()), dq, key_grad, value_grad)


def solution(mesh):
    placed = P("pipe", "ctx", None)
    return jax.shard_map(
        per_device,
        mesh=mesh,
        in_specs=(placed,) * 6 + (P(),),
        out_specs=(P(), placed, placed, placed),
        check_vma=False,
    )
```

```python
import functools
import jax
import jax.numpy as jnp
from jax import lax
from jax.experimental import pallas as pl
from jax.experimental.pallas import tpu as pltpu
from jax.sharding import PartitionSpec as P

REACH = 2
HEADS = 32
KV_HEADS = 4
HEAD_DIM = 128
GROUP = HEADS // KV_HEADS
TOK = 128
SPAN = (REACH + 1) * TOK
SPLIT = (1, 1, 2)
PARTS = len(SPLIT)
OFFSET = tuple(sum(SPLIT[:p]) for p in range(PARTS))
PAIR = 2
VMEM_LIMIT = 16 << 20
X_CHIPS = 4
RELAYED = (2,)
ORDER = (
    ("attend", 0),
    ("attend", 1),
    ("grad", 0),
    ("grad", 1),
    ("attend", 2),
    ("grad", 2),
)

NEG_FILL = -1e30
SCALE = HEAD_DIM ** (-0.5)
LOG2E = 1.4426950408889634
EXP_SCALE = SCALE * LOG2E
NT = (((1,), (1,)), ((), ()))
NN = (((1,), (0,)), ((), ()))
TN = (((0,), (0,)), ((), ()))


def mm(a, b, dims):
    return lax.dot_general(a, b, dims, preferred_element_type=jnp.float32)


def rotate(block, axis, distance):
    count = lax.axis_size(axis)
    return lax.ppermute(block, axis, [(i, (i + distance) % count) for i in range(count)])


def in_hbm(array):
    return pltpu.with_memory_space_constraint(array, pltpu.HBM)


def pack_body(pos_ref, tk, tv, sk, sv, seg0, seg1, seg2, *outs):
    packs, (bias, first_rows, first_cols) = outs[:PARTS], outs[PARTS:]
    for p in range(PARTS):
        for m, src in enumerate((tk, tv, sk, sv)):
            packs[p][m] = src[0, :, OFFSET[p] * HEAD_DIM : (OFFSET[p] + SPLIT[p]) * HEAD_DIM]
    square = lambda seg: jnp.broadcast_to(seg[0].astype(jnp.float32), (TOK, TOK))
    queries = square(seg0)
    keys0, keys1, keys2 = queries.T, square(seg1).T, square(seg2).T
    first = jnp.broadcast_to(keys0[0:1, :], (TOK, TOK))
    in_first = queries == first
    key_in_first = keys0 == first
    row = lax.broadcasted_iota(jnp.int32, (TOK, TOK), 0)
    col = lax.broadcasted_iota(jnp.int32, (TOK, TOK), 1)
    own_ok = (keys0 == queries) & (row <= col)
    near_ok = in_first & (keys1 == queries)
    far_ok = in_first & (keys2 == queries) & jnp.logical_not(key_in_first)
    bias[:TOK, :] = jnp.where(near_ok, 0.0, NEG_FILL)
    bias[TOK:, :] = jnp.where(own_ok | far_ok, 0.0, NEG_FILL)
    first_rows[...] = jnp.where(key_in_first, 1.0, 0.0)
    first_cols[...] = jnp.where(in_first, 1.0, 0.0)


def pack(pos, blocks, segment_ids):
    count = segment_ids.shape[0] // TOK
    seg = segment_ids.reshape(count, 1, TOK)
    kv = pl.BlockSpec((1, TOK, KV_HEADS * HEAD_DIM), lambda i, pos: (0, 0, 0))
    segs = [
        pl.BlockSpec((1, 1, TOK), lambda i, pos, d=d: (lax.rem(pos[0] + count - d, count), 0, 0))
        for d in range(REACH + 1)
    ]
    whole = lambda *shape: pl.BlockSpec(shape, lambda i, pos: (0,) * len(shape))
    flat = jax.ShapeDtypeStruct((TOK, TOK), jnp.float32)
    return pl.pallas_call(
        pack_body,
        grid_spec=pltpu.PrefetchScalarGridSpec(
            num_scalar_prefetch=1,
            grid=(1,),
            in_specs=[kv] * 4 + segs,
            out_specs=[whole(4, TOK, n * HEAD_DIM) for n in SPLIT] + [whole(2 * TOK, TOK)] + [whole(TOK, TOK)] * 2,
        ),
        out_shape=[jax.ShapeDtypeStruct((4, TOK, n * HEAD_DIM), jnp.bfloat16) for n in SPLIT]
        + [jax.ShapeDtypeStruct((2 * TOK, TOK), jnp.float32), flat, flat],
        compiler_params=pltpu.CompilerParams(vmem_limit_bytes=VMEM_LIMIT),
        name="pack",
    )(pos, *[in_hbm(b) for b in blocks], *[in_hbm(seg)] * 3)


def window(own, nb1, nb2, rows):
    mixed = own * rows + nb2 * (1 - rows)
    upper = jnp.concatenate([nb1, jnp.zeros_like(nb1)], axis=1)
    return jnp.concatenate([upper, jnp.concatenate([mixed, own], axis=1)], axis=0)


def query_pair(q_ref, pair, rows):
    parts = []
    for j in range(PAIR):
        h = pair * PAIR + j
        q = q_ref[0, :, h * HEAD_DIM : (h + 1) * HEAD_DIM]
        early = q * rows
        parts.append(jnp.concatenate([early, q - early], axis=1))
    return jnp.concatenate(parts, axis=0)


def forward_body(stage_ref, tq, sq, own, nb1, nb2, bias, frow, fcol, s_out, t_out, send, lse):
    ahead = stage_ref[0].astype(jnp.float32) + 1.0
    rows = frow[...].astype(jnp.bfloat16)
    early = fcol[0:1, :] > 0.5
    models = []
    for base in (0, 2):
        keys = window(own[base], nb1[base], nb2[base], rows)
        v0, v1, v2 = own[base + 1], nb1[base + 1], nb2[base + 1]
        mixed = (v0 * rows + v2 * (1 - rows)).T
        values = jnp.concatenate(
            [
                jnp.concatenate([v1.T, mixed], axis=1),
                jnp.concatenate([jnp.zeros((HEAD_DIM, TOK), jnp.bfloat16), v0.T], axis=1),
            ],
            axis=0,
        )
        models.append((keys, values))
    items = [(pair, model) for pair in range(GROUP // PAIR) for model in (0, 1)]

    def score(item):
        pair, model = item
        return mm(models[model][0], query_pair((tq, sq)[model], pair, rows), NT)

    def soften(scores):
        halves, inverses, levels = [], [], []
        for j in range(PAIR):
            s = scores[:, j * TOK : (j + 1) * TOK] + bias[...]
            peak = jnp.max(s, axis=0, keepdims=True)
            expo = jnp.exp2((s - peak) * EXP_SCALE)
            total = jnp.sum(expo, axis=0, keepdims=True)
            halves.append(expo.astype(jnp.bfloat16))
            inverses.append(1.0 / total)
            levels.append(peak * EXP_SCALE + jnp.log2(total))
        return jnp.concatenate(halves, axis=1), inverses, levels

    def mix(item, weights, inverses):
        both = mm(models[item[1]][1], weights, NN)
        outs = []
        for j in range(PAIR):
            cols = slice(j * TOK, (j + 1) * TOK)
            picked = jnp.where(early, both[:HEAD_DIM, cols], both[HEAD_DIM:, cols])
            outs.append((picked * inverses[j]).astype(jnp.bfloat16))
        return outs

    ready = score(items[0])
    teacher = None
    for n, item in enumerate(items):
        following = score(items[n + 1]) if n + 1 < len(items) else None
        weights, inverses, levels = soften(ready)
        outs = mix(item, weights, inverses)
        ready = following
        if item[1] == 0:
            teacher = outs
            continue
        for j in range(PAIR):
            h = item[0] * PAIR + j
            at = pl.ds(h * HEAD_DIM, HEAD_DIM)
            s_out[at, :] = outs[j]
            t_out[at, :] = teacher[j]
            send[at, :] = (
                outs[j].astype(jnp.float32) - ahead * teacher[j].astype(jnp.float32)
            ).astype(jnp.bfloat16)
            lse[h : h + 1, :] = levels[j]


def forward(part, stage, t_query, s_query, own, nb1, nb2, masks):
    width = GROUP * HEAD_DIM
    groups = SPLIT[part]
    total = groups * width
    query = pl.BlockSpec((1, TOK, width), lambda g, st: (0, 0, OFFSET[part] + g))
    kv = pl.BlockSpec((4, TOK, HEAD_DIM), lambda g, st: (0, 0, g))
    flipped = pl.BlockSpec((width, TOK), lambda g, st: (g, 0))
    half = jax.ShapeDtypeStruct((total, TOK), jnp.bfloat16)
    fixed = [pl.BlockSpec(m.shape, lambda g, st: (0, 0)) for m in masks]
    return pl.pallas_call(
        forward_body,
        grid_spec=pltpu.PrefetchScalarGridSpec(
            num_scalar_prefetch=1,
            grid=(groups,),
            in_specs=[query, query, kv, kv, kv] + fixed,
            out_specs=[flipped] * 3 + [pl.BlockSpec((GROUP, TOK), lambda g, st: (g, 0))],
        ),
        out_shape=[half] * 3 + [jax.ShapeDtypeStruct((groups * GROUP, TOK), jnp.float32)],
        cost_estimate=pl.CostEstimate(flops=8 * total * TOK * SPAN, bytes_accessed=6 * total * TOK * 2, transcendentals=2 * total * SPAN),
        compiler_params=pltpu.CompilerParams(vmem_limit_bytes=VMEM_LIMIT),
        name="forward",
    )(stage, in_hbm(t_query), in_hbm(s_query), own, nb1, nb2, *masks)


def backward_body(several, chained, stage_ref, sq, own, nb1, nb2, bias, frow, fcol, s_out, t_out, recv, lse, *rest):
    dq, local, back1, back2, loss, all_query, all_grad, all_prob, all_score = rest[-9:]
    stage = stage_ref[0].astype(jnp.float32)
    rows = frow[...].astype(jnp.bfloat16)
    cols_mask = fcol[...].astype(jnp.bfloat16)
    keys = window(own[0], nb1[0], nb2[0], rows)
    values = window(own[1], nb1[1], nb2[1], rows)
    width = PAIR * TOK
    squares = [jnp.zeros((8, TOK), jnp.float32)]

    def out_grad_of(h):
        at = slice(h * HEAD_DIM, (h + 1) * HEAD_DIM)
        s = s_out[at, :].astype(jnp.float32)
        t = t_out[at, :].astype(jnp.float32)
        r = recv[at, :].astype(jnp.float32)
        grad = (2.0 - stage) * (s - t) + r
        first = r - t
        both = grad * grad + first * first
        squares[0] = squares[0] + jnp.sum(both.reshape(HEAD_DIM // 8, 8, TOK), axis=0)
        half = grad.astype(jnp.bfloat16)
        return half, jnp.sum(half.astype(jnp.float32) * s, axis=0, keepdims=True)

    def start(pair):
        at = slice(pair * width, (pair + 1) * width)
        queries = query_pair(sq, pair, rows)
        all_query[at, :] = queries
        stacked, deltas = [], []
        for j in range(PAIR):
            g, delta = out_grad_of(pair * PAIR + j)
            early = g * cols_mask
            stacked.append(jnp.concatenate([early, g - early], axis=0))
            deltas.append(delta)
        out_grad = jnp.concatenate(stacked, axis=1)
        all_grad[:, at] = out_grad
        return mm(keys, queries, NT), mm(values, out_grad, NN), deltas

    ready = start(0)
    for pair in range(GROUP // PAIR):
        scores, dprob, deltas = ready
        if pair + 1 < GROUP // PAIR:
            ready = start(pair + 1)
        for j in range(PAIR):
            h = pair * PAIR + j
            part = slice(j * TOK, (j + 1) * TOK)
            at = slice(h * TOK, (h + 1) * TOK)
            prob = jnp.exp2((scores[:, part] + bias[...]) * EXP_SCALE - lse[h : h + 1, :])
            dscore = prob * (dprob[:, part] - deltas[j])
            all_prob[:, at] = prob.astype(jnp.bfloat16)
            all_score[:, at] = dscore.astype(jnp.bfloat16)
        at = slice(pair * width, (pair + 1) * width)
        query_part = mm(all_score[:, at], keys, TN)
        for j in range(PAIR):
            h = pair * PAIR + j
            both = query_part[j * TOK : (j + 1) * TOK, :]
            picked = jnp.where(frow[...] > 0.5, both[:, :HEAD_DIM], both[:, HEAD_DIM:])
            dq[0, :, h * HEAD_DIM : (h + 1) * HEAD_DIM] = picked * SCALE
    key_win = mm(all_score[...], all_query[...], NN) * SCALE
    value_win = mm(all_prob[...], all_grad[...], NT)
    for m, win in enumerate((key_win, value_win)):
        back1[m] = win[:TOK, :HEAD_DIM].astype(jnp.bfloat16)
        mixed = win[TOK:, :HEAD_DIM]
        kept = mixed * frow[...]
        back2[m] = (mixed - kept).astype(jnp.bfloat16)
        local[m] = win[TOK:, HEAD_DIM:] + kept
    total = jnp.sum(squares[0], axis=0, keepdims=True) * stage
    step = pl.program_id(0)
    before = rest[0][0:1, :] if chained else jnp.zeros((1, TOK), jnp.float32)
    if several:
        before = jnp.where(step == 0, before, loss[0:1, :])
    loss[...] = jnp.broadcast_to(total + before, loss.shape)


def backward(part, stage, s_query, own, nb1, nb2, masks, outs, recv, lse, carried, senders):
    width = GROUP * HEAD_DIM
    groups = SPLIT[part]
    total = groups * width
    last = part == PARTS - 1
    flat = senders if last else 8
    query = pl.BlockSpec((1, TOK, width), lambda g, st: (0, 0, OFFSET[part] + g))
    kv = pl.BlockSpec((2, TOK, HEAD_DIM), lambda g, st: (1, 0, g))
    flipped = pl.BlockSpec((width, TOK), lambda g, st: (g, 0))
    fixed = lambda shape: pl.BlockSpec(shape, lambda g, st: (0,) * len(shape))
    in_specs = [query, kv, kv, kv] + [fixed(m.shape) for m in masks]
    in_specs += [flipped] * 3 + [pl.BlockSpec((GROUP, TOK), lambda g, st: (g, 0))]
    args = [stage, in_hbm(s_query), own, nb1, nb2, *masks, *outs, recv, lse]
    aliases = {}
    if carried is not None:
        *buffers, squares = carried
        in_specs.append(fixed(squares.shape))
        args.append(squares)
        for n, buffer in enumerate(buffers):
            aliases[len(args)] = n
            in_specs.append(pl.BlockSpec(memory_space=pl.ANY))
            args.append(buffer)
    pair = pl.BlockSpec((2, TOK, HEAD_DIM), lambda g, st: (0, 0, OFFSET[part] + g))
    wide = (2, TOK, KV_HEADS * HEAD_DIM)
    return pl.pallas_call(
        functools.partial(backward_body, groups > 1, carried is not None),
        grid_spec=pltpu.PrefetchScalarGridSpec(
            num_scalar_prefetch=1,
            grid=(groups,),
            in_specs=in_specs,
            out_specs=[query, pair, pair, pair, fixed((flat, TOK))],
            scratch_shapes=[
                pltpu.VMEM((GROUP * TOK, 2 * HEAD_DIM), jnp.bfloat16),
                pltpu.VMEM((2 * HEAD_DIM, GROUP * TOK), jnp.bfloat16),
                pltpu.VMEM((2 * TOK, GROUP * TOK), jnp.bfloat16),
                pltpu.VMEM((2 * TOK, GROUP * TOK), jnp.bfloat16),
            ],
        ),
        out_shape=[
            jax.ShapeDtypeStruct((1, TOK, HEADS * HEAD_DIM), jnp.float32),
            jax.ShapeDtypeStruct(wide, jnp.float32),
            jax.ShapeDtypeStruct(wide, jnp.bfloat16),
            jax.ShapeDtypeStruct(wide, jnp.bfloat16),
            jax.ShapeDtypeStruct((flat, TOK), jnp.float32),
        ],
        input_output_aliases=aliases,
        cost_estimate=pl.CostEstimate(flops=10 * total * TOK * SPAN, bytes_accessed=12 * total * TOK, transcendentals=total * SPAN),
        compiler_params=pltpu.CompilerParams(vmem_limit_bytes=VMEM_LIMIT),
        name="backward",
    )(*args)


def finish_body(local, ret1, ret2, squares, loss, key_grad, value_grad):
    for m, out in enumerate((key_grad, value_grad)):
        out[0] = local[m] + ret1[m].astype(jnp.float32) + ret2[m].astype(jnp.float32)
    count = squares.shape[0] * TOK * HEADS * HEAD_DIM
    rows = jnp.sum(squares[...], axis=0, keepdims=True)
    loss[...] = jnp.sum(rows, axis=1, keepdims=True) * (1.0 / count)


def finish(local, ret1, ret2, squares):
    shape = jax.ShapeDtypeStruct((1, TOK, KV_HEADS * HEAD_DIM), jnp.float32)
    return pl.pallas_call(
        finish_body,
        out_shape=[jax.ShapeDtypeStruct((1, 1), jnp.float32), shape, shape],
        compiler_params=pltpu.CompilerParams(vmem_limit_bytes=VMEM_LIMIT),
        name="finish",
    )(local, ret1, ret2, squares)


def relay_routes(count):
    first, second = [], []
    for i in range(count):
        x = i % X_CHIPS
        first.append((i, i - 1 if x else i + X_CHIPS - 1))
        second.append((i, i - 1 if x == X_CHIPS - 1 else (i + X_CHIPS - 1) % count))
    return first, second


def per_device(t_query, t_key, t_value, s_query, s_key, s_value, segment_ids):
    pos = lax.axis_index("ctx").astype(jnp.int32).reshape(1)
    stage = lax.axis_index("pipe").astype(jnp.int32).reshape(1)
    senders = lax.axis_size("pipe") * lax.axis_size("ctx")
    packed = pack(pos, (t_key, t_value, s_key, s_value), segment_ids)
    packs, masks = packed[:PARTS], packed[PARTS:]
    near = []
    for part, block in enumerate(packs):
        nb1 = rotate(block, "ctx", 1)
        if part in RELAYED:
            first, second = relay_routes(lax.axis_size("ctx"))
            nb2 = lax.ppermute(block, "ctx", first)
            nb2 = lax.ppermute(nb2, "ctx", second)
        else:
            nb2 = rotate(block, "ctx", 2)
        near.append((nb1, nb2))
    carried = None
    token = None
    held = {}
    for kind, part in ORDER:
        own, (nb1, nb2) = packs[part], near[part]
        mark = lax.optimization_barrier((stage, token))[0] if token is not None else stage
        if kind == "attend":
            s_out, t_out, send, lse = forward(part, mark, t_query, s_query, own, nb1, nb2, masks)
            recv = rotate(send, "pipe", 1)
            held[part] = (s_out, t_out), recv, lse
            token = lse
        else:
            outs, recv, lse = held.pop(part)
            carried = backward(
                part, mark, s_query, own, nb1, nb2, masks, outs, recv, lse, carried, senders
            )
            token = carried[-1]
    dq, local, back1, back2, squares = carried
    ret1, ret2 = (rotate(back1, "ctx", -1)), (rotate(back2, "ctx", -2))
    gathered = lax.all_to_all(squares, ("ctx", "pipe"), 0, 0, tiled=True)
    loss, key_grad, value_grad = finish(local, ret1, ret2, gathered)
    return (loss.reshape(()), dq, key_grad, value_grad)


def solution(mesh):
    placed = P("pipe", "ctx", None)
    return jax.shard_map(
        per_device,
        mesh=mesh,
        in_specs=(placed,) * 6 + (P(),),
        out_specs=(P(), placed, placed, placed),
        check_vma=False,
    )
```

```python
import functools
import jax
import jax.numpy as jnp
from jax import lax
from jax.experimental import pallas as pl
from jax.experimental.pallas import tpu as pltpu
from jax.sharding import PartitionSpec as P

REACH = 2
HEADS = 32
KV_HEADS = 4
SECTIONS = 2
HEAD_DIM = 128
GROUP = HEADS // KV_HEADS
TOK = 128
SPAN = (REACH + 1) * TOK
SPLIT = (1, 1, 2)
PARTS = len(SPLIT)
OFFSET = tuple(sum(SPLIT[:p]) for p in range(PARTS))
PAIR = 2
VMEM_LIMIT = 16 << 20
X_CHIPS = 4
RELAYED = (2,)
ORDER = (
    ("attend", 0),
    ("attend", 1),
    ("grad", 0),
    ("grad", 1),
    ("attend", 2),
    ("grad", 2),
)

NEG_FILL = -1e30
SCALE = HEAD_DIM ** (-0.5)
LOG2E = 1.4426950408889634
EXP_SCALE = SCALE * LOG2E
NT = (((1,), (1,)), ((), ()))
NN = (((1,), (0,)), ((), ()))
TN = (((0,), (0,)), ((), ()))


def mm(a, b, dims):
    return lax.dot_general(a, b, dims, preferred_element_type=jnp.float32)


def rotate(block, axis, distance):
    count = lax.axis_size(axis)
    return lax.ppermute(block, axis, [(i, (i + distance) % count) for i in range(count)])


def in_hbm(array):
    return pltpu.with_memory_space_constraint(array, pltpu.HBM)


def pack_body(pos_ref, tk, tv, sk, sv, seg0, seg1, seg2, *outs):
    packs, (bias, first_rows, first_cols) = outs[:PARTS], outs[PARTS:]
    for p in range(PARTS):
        for m, src in enumerate((tk, tv, sk, sv)):
            packs[p][m] = src[0, :, OFFSET[p] * HEAD_DIM : (OFFSET[p] + SPLIT[p]) * HEAD_DIM]
    square = lambda seg: jnp.broadcast_to(seg[0].astype(jnp.float32), (TOK, TOK))
    queries = square(seg0)
    keys0, keys1, keys2 = queries.T, square(seg1).T, square(seg2).T
    first = jnp.broadcast_to(keys0[0:1, :], (TOK, TOK))
    in_first = queries == first
    key_in_first = keys0 == first
    row = lax.broadcasted_iota(jnp.int32, (TOK, TOK), 0)
    col = lax.broadcasted_iota(jnp.int32, (TOK, TOK), 1)
    own_ok = (keys0 == queries) & (row <= col)
    near_ok = in_first & (keys1 == queries)
    far_ok = in_first & (keys2 == queries) & jnp.logical_not(key_in_first)
    bias[:TOK, :] = jnp.where(near_ok, 0.0, NEG_FILL)
    bias[TOK:, :] = jnp.where(own_ok | far_ok, 0.0, NEG_FILL)
    first_rows[...] = jnp.where(key_in_first, 1.0, 0.0)
    first_cols[...] = jnp.where(in_first, 1.0, 0.0)


def pack(pos, blocks, segment_ids):
    count = segment_ids.shape[0] // TOK
    seg = segment_ids.reshape(count, 1, TOK)
    kv = pl.BlockSpec((1, TOK, KV_HEADS * HEAD_DIM), lambda i, pos: (0, 0, 0))
    segs = [
        pl.BlockSpec((1, 1, TOK), lambda i, pos, d=d: (lax.rem(pos[0] + count - d, count), 0, 0))
        for d in range(REACH + 1)
    ]
    whole = lambda *shape: pl.BlockSpec(shape, lambda i, pos: (0,) * len(shape))
    flat = jax.ShapeDtypeStruct((TOK, TOK), jnp.float32)
    return pl.pallas_call(
        pack_body,
        grid_spec=pltpu.PrefetchScalarGridSpec(
            num_scalar_prefetch=1,
            grid=(1,),
            in_specs=[kv] * 4 + segs,
            out_specs=[whole(4, TOK, n * HEAD_DIM) for n in SPLIT] + [whole(2 * TOK, TOK)] + [whole(TOK, TOK)] * 2,
        ),
        out_shape=[jax.ShapeDtypeStruct((4, TOK, n * HEAD_DIM), jnp.bfloat16) for n in SPLIT]
        + [jax.ShapeDtypeStruct((2 * TOK, TOK), jnp.float32), flat, flat],
        compiler_params=pltpu.CompilerParams(vmem_limit_bytes=VMEM_LIMIT),
        name="pack",
    )(pos, *[in_hbm(b) for b in blocks], *[in_hbm(seg)] * 3)


def window(own, nb1, nb2, rows):
    mixed = own * rows + nb2 * (1 - rows)
    upper = jnp.concatenate([nb1, jnp.zeros_like(nb1)], axis=1)
    return jnp.concatenate([upper, jnp.concatenate([mixed, own], axis=1)], axis=0)


def query_pair(q_ref, pair, rows):
    parts = []
    for j in range(PAIR):
        h = pair * PAIR + j
        q = q_ref[0, :, h * HEAD_DIM : (h + 1) * HEAD_DIM]
        early = q * rows
        parts.append(jnp.concatenate([early, q - early], axis=1))
    return jnp.concatenate(parts, axis=0)


def forward_body(stage_ref, tq, sq, own, nb1, nb2, bias, frow, fcol, s_out, t_out, send, lse):
    ahead = stage_ref[0].astype(jnp.float32) + 1.0
    rows = frow[...].astype(jnp.bfloat16)
    early = fcol[0:1, :] > 0.5
    models = []
    for base in (0, 2):
        keys = window(own[base], nb1[base], nb2[base], rows)
        v0, v1, v2 = own[base + 1], nb1[base + 1], nb2[base + 1]
        mixed = (v0 * rows + v2 * (1 - rows)).T
        values = jnp.concatenate(
            [
                jnp.concatenate([v1.T, mixed], axis=1),
                jnp.concatenate([jnp.zeros((HEAD_DIM, TOK), jnp.bfloat16), v0.T], axis=1),
            ],
            axis=0,
        )
        models.append((keys, values))
    items = [(pair, model) for pair in range(GROUP // PAIR) for model in (0, 1)]

    def score(item):
        pair, model = item
        return mm(models[model][0], query_pair((tq, sq)[model], pair, rows), NT)

    def soften(scores):
        halves, inverses, levels = [], [], []
        for j in range(PAIR):
            s = scores[:, j * TOK : (j + 1) * TOK] + bias[...]
            peak = jnp.max(s, axis=0, keepdims=True)
            expo = jnp.exp2((s - peak) * EXP_SCALE)
            total = jnp.sum(expo, axis=0, keepdims=True)
            halves.append(expo.astype(jnp.bfloat16))
            inverses.append(1.0 / total)
            levels.append(peak * EXP_SCALE + jnp.log2(total))
        return jnp.concatenate(halves, axis=1), inverses, levels

    def mix(item, weights, inverses):
        both = mm(models[item[1]][1], weights, NN)
        outs = []
        for j in range(PAIR):
            cols = slice(j * TOK, (j + 1) * TOK)
            picked = jnp.where(early, both[:HEAD_DIM, cols], both[HEAD_DIM:, cols])
            outs.append((picked * inverses[j]).astype(jnp.bfloat16))
        return outs

    ready = score(items[0])
    teacher = None
    for n, item in enumerate(items):
        following = score(items[n + 1]) if n + 1 < len(items) else None
        weights, inverses, levels = soften(ready)
        outs = mix(item, weights, inverses)
        ready = following
        if item[1] == 0:
            teacher = outs
            continue
        for j in range(PAIR):
            h = item[0] * PAIR + j
            at = pl.ds(h * HEAD_DIM, HEAD_DIM)
            s_out[at, :] = outs[j]
            t_out[at, :] = teacher[j]
            send[at, :] = (
                outs[j].astype(jnp.float32) - ahead * teacher[j].astype(jnp.float32)
            ).astype(jnp.bfloat16)
            lse[h : h + 1, :] = levels[j]


def forward(part, stage, t_query, s_query, own, nb1, nb2, masks):
    width = GROUP * HEAD_DIM
    groups = SPLIT[part]
    total = groups * width
    query = pl.BlockSpec((1, TOK, width), lambda g, st: (0, 0, OFFSET[part] + g))
    kv = pl.BlockSpec((4, TOK, HEAD_DIM), lambda g, st: (0, 0, g))
    flipped = pl.BlockSpec((width, TOK), lambda g, st: (g, 0))
    half = jax.ShapeDtypeStruct((total, TOK), jnp.bfloat16)
    fixed = [pl.BlockSpec(m.shape, lambda g, st: (0, 0)) for m in masks]
    return pl.pallas_call(
        forward_body,
        grid_spec=pltpu.PrefetchScalarGridSpec(
            num_scalar_prefetch=1,
            grid=(groups,),
            in_specs=[query, query, kv, kv, kv] + fixed,
            out_specs=[flipped] * 3 + [pl.BlockSpec((GROUP, TOK), lambda g, st: (g, 0))],
        ),
        out_shape=[half] * 3 + [jax.ShapeDtypeStruct((groups * GROUP, TOK), jnp.float32)],
        cost_estimate=pl.CostEstimate(flops=8 * total * TOK * SPAN, bytes_accessed=6 * total * TOK * 2, transcendentals=2 * total * SPAN),
        compiler_params=pltpu.CompilerParams(vmem_limit_bytes=VMEM_LIMIT),
        name="forward",
    )(stage, in_hbm(t_query), in_hbm(s_query), own, nb1, nb2, *masks)


def backward_body(several, chained, stage_ref, sq, own, nb1, nb2, bias, frow, fcol, s_out, t_out, recv, lse, *rest):
    dq, local, back1, back2, loss, all_query, all_grad, all_prob, all_score = rest[-9:]
    stage = stage_ref[0].astype(jnp.float32)
    rows = frow[...].astype(jnp.bfloat16)
    cols_mask = fcol[...].astype(jnp.bfloat16)
    keys = window(own[0], nb1[0], nb2[0], rows)
    values = window(own[1], nb1[1], nb2[1], rows)
    width = PAIR * TOK
    squares = [jnp.zeros((8, TOK), jnp.float32)]

    def out_grad_of(h):
        at = slice(h * HEAD_DIM, (h + 1) * HEAD_DIM)
        s = s_out[at, :].astype(jnp.float32)
        t = t_out[at, :].astype(jnp.float32)
        r = recv[at, :].astype(jnp.float32)
        grad = (2.0 - stage) * (s - t) + r
        first = r - t
        both = grad * grad + first * first
        squares[0] = squares[0] + jnp.sum(both.reshape(HEAD_DIM // 8, 8, TOK), axis=0)
        half = grad.astype(jnp.bfloat16)
        return half, jnp.sum(half.astype(jnp.float32) * s, axis=0, keepdims=True)

    def start(pair):
        at = slice(pair * width, (pair + 1) * width)
        queries = query_pair(sq, pair, rows)
        all_query[at, :] = queries
        stacked, deltas = [], []
        for j in range(PAIR):
            g, delta = out_grad_of(pair * PAIR + j)
            early = g * cols_mask
            stacked.append(jnp.concatenate([early, g - early], axis=0))
            deltas.append(delta)
        out_grad = jnp.concatenate(stacked, axis=1)
        all_grad[:, at] = out_grad
        return mm(keys, queries, NT), mm(values, out_grad, NN), deltas

    ready = start(0)
    for pair in range(GROUP // PAIR):
        scores, dprob, deltas = ready
        if pair + 1 < GROUP // PAIR:
            ready = start(pair + 1)
        for j in range(PAIR):
            h = pair * PAIR + j
            part = slice(j * TOK, (j + 1) * TOK)
            at = slice(h * TOK, (h + 1) * TOK)
            prob = jnp.exp2((scores[:, part] + bias[...]) * EXP_SCALE - lse[h : h + 1, :])
            dscore = prob * (dprob[:, part] - deltas[j])
            all_prob[:, at] = prob.astype(jnp.bfloat16)
            all_score[:, at] = dscore.astype(jnp.bfloat16)
        at = slice(pair * width, (pair + 1) * width)
        query_part = mm(all_score[:, at], keys, TN)
        for j in range(PAIR):
            h = pair * PAIR + j
            both = query_part[j * TOK : (j + 1) * TOK, :]
            picked = jnp.where(frow[...] > 0.5, both[:, :HEAD_DIM], both[:, HEAD_DIM:])
            dq[0, :, h * HEAD_DIM : (h + 1) * HEAD_DIM] = picked * SCALE
    key_win = mm(all_score[...], all_query[...], NN) * SCALE
    value_win = mm(all_prob[...], all_grad[...], NT)
    for m, win in enumerate((key_win, value_win)):
        back1[m] = win[:TOK, :HEAD_DIM].astype(jnp.bfloat16)
        mixed = win[TOK:, :HEAD_DIM]
        kept = mixed * frow[...]
        back2[m] = (mixed - kept).astype(jnp.bfloat16)
        local[m] = win[TOK:, HEAD_DIM:] + kept
    total = jnp.sum(squares[0], axis=0, keepdims=True) * stage
    step = pl.program_id(0)
    before = rest[0][0:1, :] if chained else jnp.zeros((1, TOK), jnp.float32)
    if several:
        before = jnp.where(step == 0, before, loss[0:1, :])
    loss[...] = jnp.broadcast_to(total + before, loss.shape)


def backward(part, stage, s_query, own, nb1, nb2, masks, outs, recv, lse, carried):
    width = GROUP * HEAD_DIM
    groups = SPLIT[part]
    total = groups * width
    flat = 8
    query = pl.BlockSpec((1, TOK, width), lambda g, st: (0, 0, OFFSET[part] + g))
    kv = pl.BlockSpec((2, TOK, HEAD_DIM), lambda g, st: (1, 0, g))
    flipped = pl.BlockSpec((width, TOK), lambda g, st: (g, 0))
    fixed = lambda shape: pl.BlockSpec(shape, lambda g, st: (0,) * len(shape))
    in_specs = [query, kv, kv, kv] + [fixed(m.shape) for m in masks]
    in_specs += [flipped] * 3 + [pl.BlockSpec((GROUP, TOK), lambda g, st: (g, 0))]
    args = [stage, in_hbm(s_query), own, nb1, nb2, *masks, *outs, recv, lse]
    aliases = {}
    if carried is not None:
        *buffers, squares = carried
        in_specs.append(fixed(squares.shape))
        args.append(squares)
        for n, buffer in enumerate(buffers):
            aliases[len(args)] = n
            in_specs.append(pl.BlockSpec(memory_space=pl.ANY))
            args.append(buffer)
    pair = pl.BlockSpec((2, TOK, HEAD_DIM), lambda g, st: (0, 0, OFFSET[part] + g))
    wide = (2, TOK, KV_HEADS * HEAD_DIM)
    return pl.pallas_call(
        functools.partial(backward_body, groups > 1, carried is not None),
        grid_spec=pltpu.PrefetchScalarGridSpec(
            num_scalar_prefetch=1,
            grid=(groups,),
            in_specs=in_specs,
            out_specs=[query, pair, pair, pair, fixed((flat, TOK))],
            scratch_shapes=[
                pltpu.VMEM((GROUP * TOK, 2 * HEAD_DIM), jnp.bfloat16),
                pltpu.VMEM((2 * HEAD_DIM, GROUP * TOK), jnp.bfloat16),
                pltpu.VMEM((2 * TOK, GROUP * TOK), jnp.bfloat16),
                pltpu.VMEM((2 * TOK, GROUP * TOK), jnp.bfloat16),
            ],
        ),
        out_shape=[
            jax.ShapeDtypeStruct((1, TOK, HEADS * HEAD_DIM), jnp.float32),
            jax.ShapeDtypeStruct(wide, jnp.float32),
            jax.ShapeDtypeStruct(wide, jnp.bfloat16),
            jax.ShapeDtypeStruct(wide, jnp.bfloat16),
            jax.ShapeDtypeStruct((flat, TOK), jnp.float32),
        ],
        input_output_aliases=aliases,
        cost_estimate=pl.CostEstimate(flops=10 * total * TOK * SPAN, bytes_accessed=12 * total * TOK, transcendentals=total * SPAN),
        compiler_params=pltpu.CompilerParams(vmem_limit_bytes=VMEM_LIMIT),
        name="backward",
    )(*args)


def finish_body(local, ret1, ret2, squares, loss, key_grad, value_grad):
    for m, out in enumerate((key_grad, value_grad)):
        out[0] = local[m] + ret1[m].astype(jnp.float32) + ret2[m].astype(jnp.float32)
    count = SECTIONS * squares.shape[0] * TOK * HEADS * HEAD_DIM
    rows = jnp.sum(squares[...], axis=0, keepdims=True)
    loss[...] = jnp.sum(rows, axis=1, keepdims=True) * (1.0 / count)


def finish(local, ret1, ret2, squares):
    shape = jax.ShapeDtypeStruct((1, TOK, KV_HEADS * HEAD_DIM), jnp.float32)
    return pl.pallas_call(
        finish_body,
        out_shape=[jax.ShapeDtypeStruct((1, 1), jnp.float32), shape, shape],
        compiler_params=pltpu.CompilerParams(vmem_limit_bytes=VMEM_LIMIT),
        name="finish",
    )(local, ret1, ret2, squares)


def relay_routes(count):
    first, second = [], []
    for i in range(count):
        x = i % X_CHIPS
        first.append((i, i - 1 if x else i + X_CHIPS - 1))
        second.append((i, i - 1 if x == X_CHIPS - 1 else (i + X_CHIPS - 1) % count))
    return first, second


def per_device(t_query, t_key, t_value, s_query, s_key, s_value, segment_ids):
    pos = lax.axis_index("ctx").astype(jnp.int32).reshape(1)
    stage = lax.axis_index("pipe").astype(jnp.int32).reshape(1)
    senders = lax.axis_size("ctx")
    packed = pack(pos, (t_key, t_value, s_key, s_value), segment_ids)
    packs, masks = packed[:PARTS], packed[PARTS:]
    near = []
    for part, block in enumerate(packs):
        nb1 = rotate(block, "ctx", 1)
        if part in RELAYED:
            first, second = relay_routes(lax.axis_size("ctx"))
            nb2 = lax.ppermute(block, "ctx", first)
            nb2 = lax.ppermute(nb2, "ctx", second)
        else:
            nb2 = rotate(block, "ctx", 2)
        near.append((nb1, nb2))
    carried = None
    token = None
    held = {}
    for kind, part in ORDER:
        own, (nb1, nb2) = packs[part], near[part]
        mark = lax.optimization_barrier((stage, token))[0] if token is not None else stage
        if kind == "attend":
            s_out, t_out, send, lse = forward(part, mark, t_query, s_query, own, nb1, nb2, masks)
            recv = rotate(send, "pipe", 1)
            held[part] = (s_out, t_out), recv, lse
            token = lse
        else:
            outs, recv, lse = held.pop(part)
            carried = backward(part, mark, s_query, own, nb1, nb2, masks, outs, recv, lse, carried)
            token = carried[-1]
    dq, local, back1, back2, squares = carried
    ret1, ret2 = (rotate(back1, "ctx", -1)), (rotate(back2, "ctx", -2))
    pooled = squares[:1] + rotate(squares, "pipe", 1)[:1]
    sent = jnp.broadcast_to(pooled, (senders, TOK))
    gathered = lax.all_to_all(sent, "ctx", 0, 0, tiled=True)
    loss, key_grad, value_grad = finish(local, ret1, ret2, gathered)
    return (loss.reshape(()), dq, key_grad, value_grad)


def solution(mesh):
    placed = P("pipe", "ctx", None)
    return jax.shard_map(
        per_device,
        mesh=mesh,
        in_specs=(placed,) * 6 + (P(),),
        out_specs=(P(), placed, placed, placed),
        check_vma=False,
    )
```
